256 devices in a mesh: space: 128 (over z, y, x), rep: 2 (over core).
Axes of the slice: x: 4, y: 4, z: 8, core: 2. Of those that a mesh axis runs over, the one named last changes fastest.
Arguments:
- features: bfloat16 [2, 512, 64, 512], P('rep', 'space'), may hold values from -6 to 6
- neighbours: int32 [2, 512, 26], P('rep', 'space'), may hold values from -1 to 35, as said below
- send_list: int32 [2, 128, 2, 16], P('rep', 'space'), may hold values from -1 to 3, as said below
- w_fine: bfloat16 [64, 1728], replicated, may hold values from -0.15625 to 0.15625
- w_down: bfloat16 [64, 512], replicated, may hold values from -0.25 to 0.25
- w_coarse: bfloat16 [64, 1728], replicated, may hold values from -0.15625 to 0.15625
- w_up: bfloat16 [64, 512], replicated, may hold values from -0.75 to 0.75
- cotangent: bfloat16 [2, 512, 64, 512], P('rep', 'space'), may hold values from -6 to 6
Outputs:
- decoded: bfloat16 [2, 512, 64, 512], P('rep', 'space')
- grad_fine: float32 [64, 1728], replicated
- grad_down: float32 [64, 512], replicated
- grad_coarse: float32 [64, 1728], replicated
- grad_up: float32 [64, 512], replicated
The draws below stay inside these ranges and needn't reach their ends.
Inputs may be any that keep to these rules, and one draw needn't show every extreme that they name: `neighbours`: A scene is a corridor 4 block positions across in the second and third dimensions; device d holds the occupied positions whose first coordinate lies in 4 d .. 4 d + 3, in Morton order. Entries follow true adjacency: below 4 a block of the same device, 4 + s (s < 4**2) the block of device d - 1 in slot s of its side 0, 4 + 4**2 + s the block of device d + 1 in slot s of its side 1, -1 an empty or outside position. In every slab the positions (0, 3, 3) and (3, 3, 3) are occupied and (3, 0, 0) is empty. send_list[d, 0, y * 4 + z] is device d's block at the last first-coordinate plane of its slab and position (y, z), send_list[d, 1, y * 4 + z] the one at the first plane; -1 where that position is empty.
All inputs are finite; a program needn't handle non-finite values.
Results may differ from the reference program's by a relative error of at most 0.007.
Values may be sent and summed in bfloat16 or wider, within the bound.
No kernel may reach another device: no remote copies, remote signals or barrier semaphores. Data moves between devices by JAX's collectives and lax.ppermute only.
A program may use at most 128 MiB of HBM per device.

```python
import jax
import jax.numpy as jnp
from jax import lax

CH = 64
EDGE = 8
BLK_DEV = 4
BLOCKS = 512
SCENES = 2


DIRECTIONS = [(a, c, e) for a in (-1, 0, 1) for c in (-1, 0, 1) for e in (-1, 0, 1) if (a, c, e) != (0, 0, 0)]


def morton(xs, ys, zs):
    return (xs & 1) << 2 | (ys & 1) << 1 | zs & 1 | (xs >> 1 & 1) << 5 | (ys >> 1 & 1) << 4 | (zs >> 1 & 1) << 3


def corridor_layout(key):
    devices = BLOCKS // BLK_DEV
    cells = jnp.arange(64, dtype=jnp.int32)
    cell_x = cells >> 2 & 1 | (cells >> 5 & 1) << 1
    cell_y = cells >> 1 & 1 | (cells >> 4 & 1) << 1
    cell_z = cells & 1 | (cells >> 3 & 1) << 1
    step_x = jnp.array([d[0] for d in DIRECTIONS], dtype=jnp.int32)
    step_y = jnp.array([d[1] for d in DIRECTIONS], dtype=jnp.int32)
    step_z = jnp.array([d[2] for d in DIRECTIONS], dtype=jnp.int32)

    def one_slab(slab_key):
        ranks = jax.random.permutation(slab_key, 64).astype(jnp.int32)
        forced = (cells == 27) | (cells == 63)
        score = jnp.where(forced, -1, jnp.where(cells == 36, 64, ranks)).astype(jnp.int32)
        order = jnp.argsort(score, stable=True).astype(jnp.int32)
        return jnp.sort(order[:BLK_DEV]).astype(jnp.int32)

    def slab_grid(chosen):
        return jnp.full((64,), -1, jnp.int32).at[chosen].set(jnp.arange(BLK_DEV, dtype=jnp.int32))

    def one_scene(scene_key):
        chosen = jax.vmap(one_slab)(jax.random.split(scene_key, devices))
        grids = jax.vmap(slab_grid)(chosen)
        empty_row = jnp.full((1, 64), -1, jnp.int32)
        lower_grids = jnp.concatenate([empty_row, grids[:-1]], axis=0).reshape(-1)
        upper_grids = jnp.concatenate([grids[1:], empty_row], axis=0).reshape(-1)
        flat_grids = grids.reshape(-1)
        new_x = jnp.take(cell_x, chosen)[:, :, None] + step_x[None, None, :]
        new_y = jnp.take(cell_y, chosen)[:, :, None] + step_y[None, None, :]
        new_z = jnp.take(cell_z, chosen)[:, :, None] + step_z[None, None, :]
        inside = (new_y >= 0) & (new_y < 4) & (new_z >= 0) & (new_z < 4)
        clip_x = jnp.clip(new_x, 0, 3)
        clip_y = jnp.clip(new_y, 0, 3)
        clip_z = jnp.clip(new_z, 0, 3)
        base = (jnp.arange(devices, dtype=jnp.int32) * 64)[:, None, None]
        local_val = jnp.take(flat_grids, base + morton(clip_x, clip_y, clip_z))
        lower_val = jnp.take(lower_grids, base + morton(3, clip_y, clip_z))
        upper_val = jnp.take(upper_grids, base + morton(0, clip_y, clip_z))
        slot = clip_y * 4 + clip_z
        same = (new_x >= 0) & (new_x < 4)
        remote = jnp.where(new_x < 0, jnp.where(lower_val >= 0, BLK_DEV + slot, -1), jnp.where(upper_val >= 0, BLK_DEV + 16 + slot, -1))
        table = jnp.where(inside, jnp.where(same, local_val, remote), -1).astype(jnp.int32)
        positions = jnp.arange(16, dtype=jnp.int32)
        upper_ids = grids[:, morton(3, positions // 4, positions % 4)]
        lower_ids = grids[:, morton(0, positions // 4, positions % 4)]
        sends = jnp.stack([upper_ids, lower_ids], axis=1).astype(jnp.int32)
        return (table.reshape(BLOCKS, 26), sends)
    scene_keys = jax.random.split(jax.random.fold_in(key, 7), SCENES)
    return jax.vmap(one_scene)(scene_keys)


def draw_neighbours(key, part):
    return corridor_layout(key)[0]


def draw_send_list(key, part):
    return corridor_layout(key)[1]


def shard_levels(rng, shape, shards, smallest, largest):
    def one(position, blocks):
        draws = jax.random.uniform(jax.random.fold_in(jax.random.fold_in(rng, 6), position), (blocks,), jnp.float32, smallest / len(shards), largest / len(shards))
        return jnp.repeat(jnp.exp(draws), shape[position] // blocks).reshape((-1,) + (1,) * (len(shape) - position - 1))

    level = one(*shards[0])
    for cut in shards[1:]:
        level = level * one(*cut)
    return level


def noise(stream_key, extent, width, bound, cuts=(), held_as=jnp.bfloat16):
    loudness = shard_levels(stream_key, extent, cuts, -0.22, 0.18) if cuts else 1.0
    entries = jax.random.normal(stream_key, extent, jnp.float32) * width * loudness
    return jnp.minimum(jnp.maximum(entries, -bound), bound).astype(held_as)


def setup_inputs(seed: int = 0) -> dict:
    streams_of = jax.random.split(jax.random.key(seed), 9)
    features = noise(streams_of[0], (SCENES, BLOCKS, CH, EDGE**3), 1.0, 6.0, ((0, 2), (1, 128)))
    neighbours = draw_neighbours(jax.random.fold_in(streams_of[8], 71), 0)
    send_list = draw_send_list(jax.random.fold_in(streams_of[8], 71), 0)
    w_fine = noise(streams_of[3], (CH, 27 * CH), (27 * CH) ** -0.5, 0.15625)
    w_down = noise(streams_of[4], (CH, 8 * CH), (8 * CH) ** -0.5, 0.25)
    w_coarse = noise(streams_of[5], (CH, 27 * CH), (27 * CH) ** -0.5, 0.15625)
    w_up = noise(streams_of[6], (CH, 8 * CH), CH ** -0.5, 0.75)
    cotangent = noise(streams_of[7], (SCENES, BLOCKS, CH, EDGE**3), 1.0, 6.0, ((0, 2), (1, 128)))
    return {"features": features, "neighbours": neighbours, "send_list": send_list, "w_fine": w_fine, "w_down": w_down, "w_coarse": w_coarse, "w_up": w_up, "cotangent": cotangent}


DIRECTIONS = [(a, c, e) for a in (-1, 0, 1) for c in (-1, 0, 1) for e in (-1, 0, 1) if (a, c, e) != (0, 0, 0)]

def silu_slope(values):
    sig = jax.nn.sigmoid(values)
    return sig * (1.0 + values * (1.0 - sig))

def source_range(step, side):
    if step < 0:
        return slice(side - 1, side)
    if step == 0:
        return slice(0, side)
    return slice(0, 1)

def target_range(step, side):
    if step < 0:
        return slice(0, 1)
    if step == 0:
        return slice(1, side + 1)
    return slice(side + 1, side + 2)

def assemble(own_blocks, combined, sources, side):
    count, channels = (own_blocks.shape[0], own_blocks.shape[1])
    cubes = combined.reshape(combined.shape[0], channels, side, side, side)
    padded = jnp.zeros((count, channels, side + 2, side + 2, side + 2), own_blocks.dtype)
    padded = padded.at[:, :, 1:side + 1, 1:side + 1, 1:side + 1].set(own_blocks.reshape(count, channels, side, side, side))
    for k, (a, c, e) in enumerate(DIRECTIONS):
        part_cells = cubes[:, :, source_range(a, side), source_range(c, side), source_range(e, side)]
        source_ids = sources[:, k]
        gathered = jnp.take(part_cells, jnp.maximum(source_ids, 0), axis=0)
        gathered = jnp.where((source_ids >= 0)[:, None, None, None, None], gathered, jnp.zeros_like(gathered))
        padded = padded.at[:, :, target_range(a, side), target_range(c, side), target_range(e, side)].set(gathered)
    return padded

def lattice_columns(padded, side):
    count, channels = (padded.shape[0], padded.shape[1])
    parts_list = [padded[:, :, a:a + side, c:c + side, e:e + side].reshape(count, channels, side ** 3) for a in range(3) for c in range(3) for e in range(3)]
    return jnp.concatenate(parts_list, axis=1)

def spread_back(back_cols, side):
    count = back_cols.shape[0]
    channels = back_cols.shape[1] // 27
    result = jnp.zeros((count, channels, side + 2, side + 2, side + 2), back_cols.dtype)
    for a in range(3):
        for c in range(3):
            for e in range(3):
                offset = 9 * a + 3 * c + e
                piece = back_cols[:, offset * channels:(offset + 1) * channels].reshape(count, channels, side, side, side)
                result = result.at[:, :, a:a + side, c:c + side, e:e + side].add(piece)
    return result

def to_patches(field, side):
    count, channels = (field.shape[0], field.shape[1])
    half = side // 2
    shaped = field.reshape(count, channels, half, 2, half, 2, half, 2).transpose(0, 3, 5, 7, 1, 2, 4, 6)
    return shaped.reshape(count, 8 * channels, half ** 3)

def from_patches(values, half):
    count = values.shape[0]
    channels = values.shape[1] // 8
    shaped = values.reshape(count, 2, 2, 2, channels, half, half, half).transpose(0, 4, 5, 1, 6, 2, 7, 3)
    return shaped.reshape(count, channels, 8 * half ** 3)

def apply_conv(weight, halo, side):
    count = halo.shape[0]
    grouped = halo.reshape((count // 16, 16) + halo.shape[1:])

    def conv_step(pad_group):
        return jnp.einsum('ok,gkv->gov', weight.astype(jnp.float32), lattice_columns(pad_group, side).astype(jnp.float32))
    return lax.map(conv_step, grouped).reshape(count, weight.shape[0], side ** 3)

def conv_weights(delta, halo, side):
    count = halo.shape[0]
    channels = halo.shape[1]
    grouped = halo.reshape((count // 16, 16) + halo.shape[1:])
    delta_groups = delta.reshape((count // 16, 16) + delta.shape[1:])

    def weight_step(total, pair):
        pad_group, delta_group = pair
        cols = lattice_columns(pad_group, side).astype(jnp.float32)
        return (total + jnp.einsum('gov,gkv->ok', delta_group.astype(jnp.float32), cols), None)
    total, _ = lax.scan(weight_step, jnp.zeros((channels, 27 * channels), jnp.float32), (grouped, delta_groups))
    return total

def apply_adjoint(weight, delta, side):
    count = delta.shape[0]
    delta_groups = delta.reshape((count // 16, 16) + delta.shape[1:])

    def adjoint_step(delta_group):
        back_cols = jnp.einsum('ok,gov->gkv', weight.astype(jnp.float32), delta_group.astype(jnp.float32))
        return spread_back(back_cols, side)
    result = lax.map(adjoint_step, delta_groups)
    return result.reshape((count,) + result.shape[2:])

def halo_adjoint(back_pad, sources, side):
    count, channels = (back_pad.shape[0], back_pad.shape[1])
    totals = jnp.zeros((count + 1, channels, side, side, side), back_pad.dtype)
    for k, (a, c, e) in enumerate(DIRECTIONS):
        piece = back_pad[:, :, target_range(a, side), target_range(c, side), target_range(e, side)]
        source_ids = jnp.where(sources[:, k] >= 0, sources[:, k], count).astype(jnp.int32)
        totals = totals.at[source_ids, :, source_range(a, side), source_range(c, side), source_range(e, side)].add(piece)
    centre = back_pad[:, :, 1:side + 1, 1:side + 1, 1:side + 1]
    return (centre + totals[:count]).reshape(count, channels, side ** 3)

def global_sources(table, sends):
    devices = BLOCKS // BLK_DEV
    slots = sends.shape[2]
    owner = (jnp.arange(BLOCKS, dtype=jnp.int32) // BLK_DEV)[:, None]
    remote = jnp.clip(table - BLK_DEV, 0, 2 * slots - 1).astype(jnp.int32)
    side_id = remote // slots
    slot_id = remote % slots
    peer = jnp.clip(owner - 1 + 2 * side_id, 0, devices - 1).astype(jnp.int32)
    remote_id = peer * BLK_DEV + sends[peer, side_id, slot_id]
    local_id = owner * BLK_DEV + table
    return jnp.where(table < 0, -1, jnp.where(table < BLK_DEV, local_id, remote_id)).astype(jnp.int32)

def reference(features, neighbours, send_list, w_fine, w_down, w_coarse, w_up, cotangent):
    f32 = jnp.float32
    coarse_side = EDGE // 2
    channels = w_fine.shape[0]
    grad_fine = jnp.zeros((channels, 27 * channels), f32)
    grad_down = jnp.zeros((channels, 8 * channels), f32)
    grad_coarse = jnp.zeros((channels, 27 * channels), f32)
    grad_up = jnp.zeros((channels, 8 * channels), f32)
    decoded_list = []
    for scene in range(SCENES):
        sources = global_sources(neighbours[scene], send_list[scene])
        fine_in = features[scene]
        halo0 = assemble(fine_in, fine_in, sources, EDGE)
        fine_pre = apply_conv(w_fine, halo0, EDGE)
        hidden0 = jax.nn.silu(fine_pre).astype(jnp.bfloat16)
        patches0 = to_patches(hidden0, EDGE)
        coarse_pre = jnp.einsum('ok,bkv->bov', w_down.astype(f32), patches0.astype(f32))
        hidden1 = jax.nn.silu(coarse_pre).astype(jnp.bfloat16)
        halo1 = assemble(hidden1, hidden1, sources, coarse_side)
        coarse_conv = apply_conv(w_coarse, halo1, coarse_side)
        gated = jax.nn.silu(coarse_conv).astype(jnp.bfloat16)
        up_terms = from_patches(jnp.einsum('ik,biv->bkv', w_up.astype(f32), gated.astype(f32)), coarse_side)
        decoded_list.append((hidden0.astype(f32) + up_terms).astype(jnp.bfloat16))
        cot_patch = to_patches(cotangent[scene], EDGE).astype(f32)
        grad_up = grad_up + jnp.einsum('biv,bkv->ik', gated.astype(f32), cot_patch)
        up_back = jnp.einsum('ik,bkv->biv', w_up.astype(f32), cot_patch)
        delta_up = (up_back * silu_slope(coarse_conv)).astype(jnp.bfloat16)
        grad_coarse = grad_coarse + conv_weights(delta_up, halo1, coarse_side)
        back_pad = apply_adjoint(w_coarse, delta_up, coarse_side)
        grad_hidden1 = halo_adjoint(back_pad, sources, coarse_side)
        delta_down = (grad_hidden1 * silu_slope(coarse_pre)).astype(jnp.bfloat16)
        grad_down = grad_down + jnp.einsum('bov,bkv->ok', delta_down.astype(f32), patches0.astype(f32))
        down_back = jnp.einsum('ok,bov->bkv', w_down.astype(f32), delta_down.astype(f32))
        grad_hidden0 = cotangent[scene].astype(f32) + from_patches(down_back, coarse_side)
        delta_fine = (grad_hidden0 * silu_slope(fine_pre)).astype(jnp.bfloat16)
        grad_fine = grad_fine + conv_weights(delta_fine, halo0, EDGE)
    factor = 1.0 / jnp.sqrt(jnp.asarray(SCENES * BLOCKS * EDGE ** 3, f32))
    return (jnp.stack(decoded_list), grad_fine * factor, grad_down * factor, grad_coarse * factor, grad_up * factor)
```

```python
import math

import jax
import jax.numpy as jnp
import numpy as np
from jax import lax
from jax.experimental import pallas as pl
from jax.experimental.pallas import tpu as pltpu
from jax.sharding import PartitionSpec as P

F32 = jnp.float32
BF16 = jnp.bfloat16
I32 = jnp.int32
AXES = ("space", "rep")
FINE_SHIFTS = [10 * (c - 1) + (e - 1) for c in range(3) for e in range(3)]
COARSE_SHIFTS = [6 * (c - 1) + (e - 1) for c in range(3) for e in range(3)]


def lane_tables():
    table = np.full((16, 2048), -1, np.int32)
    t = np.arange(128)
    y, z, inside = t // 10 - 1, t % 10 - 1, t < 100
    c, e = np.where(y < 0, 0, np.where(y >= 8, 2, 1)), np.where(z < 0, 0, np.where(z >= 8, 2, 1))
    table[0, :128] = np.where(inside, 3 * c + e, -1)
    table[1, :128] = np.where(inside, (y - 8 * (c - 1)) * 8 + (z - 8 * (e - 1)), 0)
    own = inside & (c == 1) & (e == 1)
    for b in range(4):
        table[4, 128 * b : 128 * b + 128] = np.where(own, 64 * b + y * 8 + z, -1)
    u = np.arange(64)
    cy, cz, cin = u // 6 - 1, u % 6 - 1, u < 36
    cc, ce = np.where(cy < 0, 0, np.where(cy >= 4, 2, 1)), np.where(cz < 0, 0, np.where(cz >= 4, 2, 1))
    for b in range(2):
        at = slice(64 * b, 64 * b + 64)
        table[2, at] = np.where(cin, 3 * cc + ce, -1)
        table[3, at] = np.where(cin, 6 * (cy - 4 * (cc - 1) + 1) + cz - 4 * (ce - 1) + 1, 0)
    cown = cin & (cc == 1) & (ce == 1)
    w = np.arange(64)
    for j in range(2):
        for l in range(2):
            for b in range(2):
                at = (2 * j + l) * 128 + 64 * b
                rows = 128 * b + 10 * (2 * cy + j + 1) + 2 * cz + l + 1
                table[5, at : at + 64] = np.where(cown, rows, -1)
            for b in range(4):
                ny, nz = w // 8, w % 8
                hit = (ny % 2 == j) & (nz % 2 == l)
                at = (2 * j + l) * 256 + 64 * b
                table[7, at : at + 64] = np.where(hit, 64 * b + 6 * (ny // 2 + 1) + nz // 2 + 1, -1)
                hit = own & (y % 2 == j) & (z % 2 == l)
                at = (2 * j + l) * 512 + 128 * b
                table[8, at : at + 128] = np.where(hit, 64 * b + 6 * (y // 2 + 1) + z // 2 + 1, -1)
    for b in range(2):
        table[6, 64 * b : 64 * b + 64] = 128 * b + 10 * (w // 8 + 1) + w % 8 + 1
    return table


TABLE = lane_tables()


def mm(a, b):
    return jnp.dot(a, b, preferred_element_type=F32)


def nt(a, b):
    return lax.dot_general(a, b, (((1,), (1,)), ((), ())), preferred_element_type=F32)


def roll(v, shift):
    return pltpu.roll(v, shift % 128, 1)


def onehot(code, rows):
    hit = lax.broadcasted_iota(I32, (rows, code.shape[1]), 0) == code
    return jnp.where(hit, 1.0, 0.0).astype(BF16)


def low_half(shape):
    return lax.broadcasted_iota(I32, shape, 1) < 64


def merge(low, first, second):
    return jnp.where(low, first, roll(second, 64))


def merge_high(low, first, second):
    return jnp.where(low, roll(first, 64), second)


def sigmoid(v):
    return 1.0 / (1.0 + jnp.exp(-v))


def silu(v):
    return v / (1.0 + jnp.exp(-v))


def slope(v):
    s = sigmoid(v)
    return s * (1.0 + v * (1.0 - s))


def raw_slots(neighbours, a, block, direction):
    found = jnp.full(direction.shape, -1, I32)
    for j in range(9):
        k = 9 * a + j
        entry = block if k == 13 else neighbours[block, k - (k > 13)]
        found = jnp.where(direction == j, entry, found)
    return found


def local_code(slots, cells):
    return jnp.where(slots >= 0, slots * 64 + cells, -1)


def edge_code(slots, cells, base, remote_slots):
    code = jnp.where((slots >= 0) & (slots < 4), slots * 64 + cells, -1)
    reach = (slots >= base) & (slots < base + 16)
    for j in range(4):
        hit = reach & (slots - base == remote_slots[j : j + 1])
        code = jnp.where(hit, 256 + j * 64 + cells, code)
    return code


def fine_slots(neighbours, table, a):
    direction = table[0:1, :128]
    return [raw_slots(neighbours, a, b, direction) for b in range(4)]


def coarse_slots(neighbours, table, a):
    direction = table[2:3, :128]
    low = low_half((1, 128))
    per_block = [raw_slots(neighbours, a, b, direction) for b in range(4)]
    return [jnp.where(low, per_block[0], per_block[1]), jnp.where(low, per_block[2], per_block[3])]


def arrived_slots(payload):
    return payload[128:144, :].astype(F32).astype(I32)


def tap_rows(w_ref):
    return jnp.concatenate([w_ref[:, 576 * a : 576 * a + 576] for a in range(3)], axis=0)


def put_taps(dst, at, plane, shifts):
    for s in range(plane.shape[1] // 128):
        piece = plane[:, 128 * s : 128 * s + 128]
        for j, shift in enumerate(shifts):
            moved = piece if shift == 0 else roll(piece, -shift)
            dst[64 * j : 64 * j + 64, at + 128 * s : at + 128 * s + 128] = moved


def natural_planes(ref):
    low = low_half((64, 128))
    planes = []
    for t in range(4):
        tiles = [ref[b, :, 128 * t : 128 * t + 128] for b in range(4)]
        planes.append(jnp.concatenate([merge(low, tiles[2 * p], tiles[2 * p + 1]) for p in range(2)], axis=1))
        planes.append(jnp.concatenate([merge_high(low, tiles[2 * p], tiles[2 * p + 1]) for p in range(2)], axis=1))
    return planes


def transposed_blocks(w, order):
    wt = w.astype(F32).T
    return jnp.concatenate([wt[64 * k : 64 * k + 64, :] for k in order], axis=1).astype(BF16)


def pack_faces(sends, low_tile, high_tile, to_upper, to_lower):
    low = low_half((64, 128))
    for p in range(2):
        to_upper[64 * p : 64 * p + 64, :] = merge_high(low, high_tile[2 * p], high_tile[2 * p + 1])
        to_lower[64 * p : 64 * p + 64, :] = merge(low, low_tile[2 * p], low_tile[2 * p + 1])
    rows = lax.broadcasted_iota(I32, (16, 128), 0)
    for side, out in ((0, to_upper), (1, to_lower)):
        slots = jnp.full((16, 128), -1, I32)
        for j in range(4):
            slot = jnp.int32(-1)
            for s in range(16):
                slot = jnp.where(sends[side, s] == j, s, slot)
            slots = jnp.where(rows == j, slot, slots)
        out[128:144, :] = slots.astype(F32).astype(BF16)


def fine_inner(neighbours, table, feat, cot, w_fine, w_up, w_down, w_coarse,
               pre, ext, edges, cot_plane, cot_patch, up_back, w_adj, w_ups, w_dns, taps):
    planes = natural_planes(feat)
    edges[0], edges[1] = planes[0], planes[7]
    cells = table[1:2, :128]
    code = jnp.concatenate([local_code(v, cells) for v in fine_slots(neighbours, table, 1)], axis=1)
    whole = mm(jnp.concatenate(planes, axis=0), onehot(code, 256)).astype(BF16)
    weight = tap_rows(w_fine)
    for x in range(8):
        plane = whole[64 * x : 64 * x + 64]
        ext[x] = plane
        put_taps(taps, 512 * x, plane, FINE_SHIFTS)
    for x in range(8):
        part = mm(weight, taps[:, 512 * x : 512 * x + 512])
        for a in range(3):
            out = x + 1 - a
            if 0 <= out < 8:
                piece = part[64 * a : 64 * a + 64]
                if x == max(out - 1, 0):
                    pre[out] = piece
                else:
                    pre[out] += piece
    placed = mm(jnp.concatenate(natural_planes(cot), axis=0), onehot(table[4:5, :512], 256)).astype(BF16)
    for x in range(8):
        cot_plane[x] = placed[64 * x : 64 * x + 64]
    down = onehot(table[5:6, :512], 256)
    for p in range(2):
        put_patches(cot_patch, mm(placed[:, 256 * p : 256 * p + 256], down).astype(BF16), p)
    up_back[...] = mm(w_up[...], cot_patch[...])
    for a in range(3):
        order = [(2 - a) * 9 + 8 - j for j in range(9)]
        w_adj[64 * a : 64 * a + 64, :] = transposed_blocks(w_coarse[...], order)
    for i in range(2):
        w_ups[64 * i : 64 * i + 64, :] = transposed_blocks(w_up[...], range(4 * i, 4 * i + 4))
        w_dns[64 * i : 64 * i + 64, :] = transposed_blocks(w_down[...], range(4 * i, 4 * i + 4))


def put_patches(dst, selected, pair):
    for x in range(8):
        for jl in range(4):
            at = ((x % 2) * 4 + jl) * 64
            lane = (x // 2) * 256 + pair * 128
            dst[at : at + 64, lane : lane + 128] = selected[64 * x : 64 * x + 64, 128 * jl : 128 * jl + 128]


def fine_outer(neighbours, table, from_lower, from_upper, edges, pre, w_fine, w_down,
               hidden, patch, coarse_pre, hidden1, pre_edge, ext_edge, taps):
    cells = table[1:2, :128]
    weight = tap_rows(w_fine)
    for side, a, base, payload in ((0, 0, 4, from_lower), (1, 2, 20, from_upper)):
        slots = arrived_slots(payload)
        code = jnp.concatenate([edge_code(v, cells, base, slots) for v in fine_slots(neighbours, table, a)], axis=1)
        pool = jnp.concatenate([edges[1 - side], payload[0:64, :], payload[64:128, :]], axis=1)
        plane = mm(pool, onehot(code, 512)).astype(BF16)
        ext_edge[side] = plane
        put_taps(taps, 512 * side, plane, FINE_SHIFTS)
        part = mm(weight[64 * a : 64 * a + 64], taps[:, 512 * side : 512 * side + 512])
        pre_edge[side] = pre[7 * side] + part
    for x in range(8):
        value = pre_edge[0] if x == 0 else pre_edge[1] if x == 7 else pre[x]
        hidden[x] = silu(value).astype(BF16)
    down = onehot(table[5:6, :512], 256)
    for p in range(2):
        rows = jnp.concatenate([hidden[x, :, 256 * p : 256 * p + 256] for x in range(8)], axis=0)
        put_patches(patch, mm(rows, down).astype(BF16), p)
    value = mm(w_down[...], patch[...])
    coarse_pre[...] = value
    hidden1[...] = silu(value).astype(BF16)


def by_rows(v):
    return jnp.concatenate([v[:, 256 * x : 256 * x + 256] for x in range(4)], axis=0)


def coarse_inner_conv(field, select, weight, taps, ext):
    whole = mm(by_rows(field), select).astype(BF16)
    for x in range(4):
        plane = whole[64 * x : 64 * x + 64]
        if ext is not None:
            ext[:, 256 * x : 256 * x + 256] = plane
        put_taps(taps, 256 * x, plane, COARSE_SHIFTS)
    part = mm(weight, taps[:, :1024])
    sums = []
    for x in range(4):
        total = part[64:128, 256 * x : 256 * x + 256]
        if x > 0:
            total = total + part[0:64, 256 * x - 256 : 256 * x]
        if x < 3:
            total = total + part[128:192, 256 * x + 256 : 256 * x + 512]
        sums.append(total)
    return jnp.concatenate(sums, axis=1)


def coarse_outer_conv(codes, side, own_plane, arrived, weight, taps, at):
    pool = jnp.concatenate([own_plane, arrived], axis=1)
    plane = mm(pool, onehot(codes[side : side + 1, :], 512)).astype(BF16)
    put_taps(taps, at, plane, COARSE_SHIFTS)
    return mm(weight[128 * side : 128 * side + 64], taps[:, at : at + 256]), plane


def coarse_inner(neighbours, table, from_lower, from_upper, hidden1, pre, pre_edge, w_coarse,
                 codes, ext, conv, fine_slope, taps):
    cells = table[3:4, :128]
    for row, a, base, payload in ((0, 0, 4, from_lower), (1, 2, 20, from_upper)):
        slots = arrived_slots(payload)
        code = [edge_code(v, cells, base, slots) for v in coarse_slots(neighbours, table, a)]
        codes[row : row + 1, :] = jnp.concatenate(code, axis=1)
    code = [local_code(v, cells) for v in coarse_slots(neighbours, table, 1)]
    codes[2:3, :] = jnp.concatenate(code, axis=1)
    codes[3:8, :] = jnp.full((5, 256), -1, I32)
    select = onehot(codes[2:3, :], 256)
    conv[...] = coarse_inner_conv(hidden1[...], select, tap_rows(w_coarse), taps, ext)
    for x in range(8):
        value = pre_edge[0] if x == 0 else pre_edge[1] if x == 7 else pre[x]
        fine_slope[x] = slope(value)


def coarse_outer(codes, hidden1, from_lower, from_upper, conv, up_back, w_coarse,
                 gated, delta, ext_edge, taps):
    weight = tap_rows(w_coarse)
    low, ext_edge[0] = coarse_outer_conv(codes, 0, hidden1[:, 768:], from_lower[...], weight, taps, 0)
    high, ext_edge[1] = coarse_outer_conv(codes, 1, hidden1[:, :256], from_upper[...], weight, taps, 256)
    value = conv[...]
    value = jnp.concatenate([value[:, :256] + low, value[:, 256:768], value[:, 768:] + high], axis=1)
    gated[...] = silu(value).astype(BF16)
    delta[...] = (up_back[...] * slope(value)).astype(BF16)


def decode(table, codes, gated, hidden, delta, cot_patch, ext, ext_edge, w_ups, w_adj,
           decoded, grads, back, taps, stack, spread):
    select = onehot(codes[2:3, :], 256)
    back[...] = coarse_inner_conv(delta[...], select, w_adj[...], taps, None)
    chosen = mm(by_rows(gated[...]), onehot(table[7:8, :1024], 256)).astype(BF16)
    for x in range(4):
        for jl in range(4):
            spread[64 * jl : 64 * jl + 64, 256 * x : 256 * x + 256] = (
                chosen[64 * x : 64 * x + 64, 256 * jl : 256 * jl + 256]
            )
    up = mm(w_ups[...], spread[...])
    compress = onehot(table[6:7, :128], 256)
    low = low_half((64, 128))
    for p in range(2):
        rows = jnp.concatenate([hidden[x, :, 256 * p : 256 * p + 256] for x in range(8)], axis=0)
        own = mm(rows, compress)
        for t in range(4):
            even, odd = [
                own[64 * x : 64 * x + 64] + up[64 * i : 64 * i + 64, 256 * t + 128 * p : 256 * t + 128 * p + 128]
                for i, x in ((0, 2 * t), (1, 2 * t + 1))
            ]
            decoded[2 * p, :, 128 * t : 128 * t + 128] = merge(low, even, odd).astype(BF16)
            decoded[2 * p + 1, :, 128 * t : 128 * t + 128] = merge_high(low, even, odd).astype(BF16)
    put_taps(taps, 0, ext_edge[0], COARSE_SHIFTS)
    for x in range(4):
        put_taps(taps, 256 + 256 * x, ext[:, 256 * x : 256 * x + 256], COARSE_SHIFTS)
    put_taps(taps, 1280, ext_edge[1], COARSE_SHIFTS)
    stack[...] = jnp.zeros(stack.shape, BF16)
    for a in range(3):
        stack[64 * a : 64 * a + 64, 256 * a : 256 * a + 1024] = delta[...]
    of_coarse = nt(taps[...], stack[...])
    of_up = jnp.concatenate([nt(cot_patch[...], gated[...]), jnp.zeros((64, 64), F32)], axis=0)
    grads[...] = jnp.concatenate([of_coarse, of_up], axis=1)


def finish(table, codes, delta, from_lower, from_upper, back, w_adj, coarse_pre, patch, w_dns, fine_slope,
           cot_plane, ext, ext_edge, grads, coarse_taps, spread, taps, stack):
    weight = w_adj[...]
    low, _ = coarse_outer_conv(codes, 0, delta[:, 768:], from_lower[...], weight, coarse_taps, 0)
    high, _ = coarse_outer_conv(codes, 1, delta[:, :256], from_upper[...], weight, coarse_taps, 256)
    value = back[...]
    value = jnp.concatenate([value[:, :256] + low, value[:, 256:768], value[:, 768:] + high], axis=1)
    down = (value * slope(coarse_pre[...])).astype(BF16)
    of_down = jnp.concatenate([nt(patch[...], down), jnp.zeros((64, 64), F32)], axis=0)
    chosen = mm(by_rows(down), onehot(table[8:9, :2048], 256)).astype(BF16)
    for x in range(4):
        for jl in range(4):
            spread[64 * jl : 64 * jl + 64, 512 * x : 512 * x + 512] = (
                chosen[64 * x : 64 * x + 64, 512 * jl : 512 * jl + 512]
            )
    for a in range(3):
        for plane in range(10):
            if not 0 <= plane - a < 8:
                stack[64 * a : 64 * a + 64, 512 * plane : 512 * plane + 512] = jnp.zeros((64, 512), BF16)
    for half in range(4):
        raised = mm(w_dns[...], spread[:, 512 * half : 512 * half + 512])
        for i in range(2):
            x = 2 * half + i
            total = cot_plane[x].astype(F32) + raised[64 * i : 64 * i + 64]
            fine = (total * fine_slope[x]).astype(BF16)
            for a in range(3):
                at = 512 * (x + a)
                stack[64 * a : 64 * a + 64, at : at + 512] = fine
    put_taps(taps, 0, ext_edge[0], FINE_SHIFTS)
    for x in range(8):
        put_taps(taps, 512 * x + 512, ext[x], FINE_SHIFTS)
    put_taps(taps, 4608, ext_edge[1], FINE_SHIFTS)
    grads[...] = jnp.concatenate([nt(taps[...], stack[...]), of_down], axis=1)


def unfold(factor, total, grad_fine, grad_down, grad_coarse, grad_up):
    for at, wide, narrow in ((0, grad_fine, grad_down), (256, grad_coarse, grad_up)):
        turned = (total[:, at : at + 256].astype(F32) * factor).T
        wide[...] = jnp.concatenate([turned[64 * a : 64 * a + 64, :] for a in range(3)], axis=1)
        narrow[...] = turned[192:256, :512]


VMEM_SPEC = pl.BlockSpec(memory_space=pltpu.VMEM)
SMEM_SPEC = pl.BlockSpec(memory_space=pltpu.SMEM)


def call(kernel, name, outs, scratch, *args):
    specs = [SMEM_SPEC if a.dtype == I32 and a.shape in ((4, 26), (2, 16)) else VMEM_SPEC for a in args]
    return pl.pallas_call(
        kernel,
        name=name,
        out_shape=[jax.ShapeDtypeStruct(s, t) for s, t in outs],
        in_specs=specs,
        out_specs=[VMEM_SPEC] * len(outs),
        scratch_shapes=[pltpu.VMEM(s, t) for s, t in scratch],
        compiler_params=pltpu.CompilerParams(vmem_limit_bytes=40 * 1024 * 1024),
    )(*args)


def passed_along(block, distance):
    devices = range(lax.axis_size("space"))
    route = [(i - distance, i) for i in devices if i - distance in devices]
    return lax.ppermute(block, "space", route)


def gray(i):
    return i ^ (i >> 1)


def ungray(g):
    i = 0
    while g:
        i ^= g
        g >>= 1
    return i


def stages(count):
    fields, offset, left = [], 0, count.bit_length() - 1
    for width in (1, 2, 2, 3):
        width = min(width, left)
        if width:
            fields.append((offset, width))
        offset, left = offset + width, left - width
    return [(offset, width, bit) for offset, width in fields for bit in range(width)]


def swap(x, stage):
    offset, width, bit = stage
    count = lax.axis_size(AXES)
    mask = ((1 << width) - 1) << offset
    pairs = []
    for i in range(count):
        other = ungray(gray((i & mask) >> offset) ^ (1 << bit))
        pairs.append((i, (i & ~mask) | (other << offset)))
    return lax.ppermute(x, AXES, pairs)


def my_bit(stage):
    offset, width, bit = stage
    place = (lax.axis_index(AXES) >> offset) & ((1 << width) - 1)
    return (gray(place) >> bit) & 1


def total_over_devices(x):
    todo = stages(lax.axis_size(AXES))
    split, whole = todo[:3], todo[3:]
    for stage in split:
        half = x.shape[0] // 2
        mine = my_bit(stage)
        keep = lax.dynamic_slice_in_dim(x, mine * half, half, 0)
        send = lax.dynamic_slice_in_dim(x, (1 - mine) * half, half, 0)
        x = keep.astype(F32) + swap(send.astype(BF16), stage).astype(F32)
    for stage in whole:
        rounded = x.astype(BF16)
        x = rounded.astype(F32) + swap(rounded, stage).astype(F32)
    x = x.astype(BF16)
    for stage in split[::-1]:
        first = my_bit(stage) == 0
        other = swap(x, stage)
        x = jnp.concatenate([jnp.where(first, x, other), jnp.where(first, other, x)], axis=0)
    return x


def shards(features, neighbours, send_list, w_fine, w_down, w_coarse, w_up, cotangent):
    feat, cot = features[0], cotangent[0]
    near, sends = neighbours[0], send_list[0, 0]
    table = jnp.asarray(TABLE)
    tile = (4, 64, 128)
    face = jax.ShapeDtypeStruct((144, 128), BF16)
    to_upper, to_lower = pl.pallas_call(
        pack_faces,
        name="pack_faces",
        grid=(1,),
        out_shape=[face, face],
        in_specs=[SMEM_SPEC, pl.BlockSpec(tile, lambda i: (0, 0, 0)), pl.BlockSpec(tile, lambda i: (0, 0, 3))],
        out_specs=[pl.BlockSpec((144, 128), lambda i: (0, 0))] * 2,
    )(sends, feat, feat)
    from_lower, from_upper = passed_along(to_upper, 1), passed_along(to_lower, -1)

    fine = (8, 64, 512)
    pre, ext0, edges, cot_plane, cot_patch, up_back, w_adj, w_ups, w_dns = call(
        fine_inner, "fine_inner",
        [(fine, F32), (fine, BF16), ((2, 64, 256), BF16), (fine, BF16), ((512, 1024), BF16), ((64, 1024), F32),
         ((192, 576), BF16), ((128, 256), BF16), ((128, 256), BF16)],
        [((576, 4096), BF16)],
        near, table, feat, cot, w_fine, w_up, w_down, w_coarse,
    )
    hidden0, patch0, coarse_pre, hidden1, pre_edge, ext0_edge = call(
        fine_outer, "fine_outer",
        [(fine, BF16), ((512, 1024), BF16), ((64, 1024), F32), ((64, 1024), BF16), ((2, 64, 512), F32),
         ((2, 64, 512), BF16)],
        [((576, 1024), BF16)],
        near, table, from_lower, from_upper, edges, pre, w_fine, w_down,
    )
    low1, high1 = passed_along(hidden1[:, 768:], 1), passed_along(hidden1[:, :256], -1)
    codes, ext1, conv, fine_slope = call(
        coarse_inner, "coarse_inner",
        [((8, 256), I32), ((64, 1024), BF16), ((64, 1024), F32), (fine, F32)],
        [((576, 1024), BF16)],
        near, table, from_lower, from_upper, hidden1, pre, pre_edge, w_coarse,
    )
    gated, delta_up, ext1_edge = call(
        coarse_outer, "coarse_outer",
        [((64, 1024), BF16), ((64, 1024), BF16), ((2, 64, 256), BF16)],
        [((576, 512), BF16)],
        codes, hidden1, low1, high1, conv, up_back, w_coarse,
    )
    low2, high2 = passed_along(delta_up[:, 768:], 1), passed_along(delta_up[:, :256], -1)
    decoded, grads_b, back = call(
        decode, "decode",
        [((4, 64, 512), BF16), ((576, 256), F32), ((64, 1024), F32)],
        [((576, 1536), BF16), ((192, 1536), BF16), ((256, 1024), BF16)],
        table, codes, gated, hidden0, delta_up, cot_patch, ext1, ext1_edge, w_ups, w_adj,
    )
    (grads_a,) = call(
        finish, "finish",
        [((576, 256), F32)],
        [((576, 512), BF16), ((256, 2048), BF16), ((576, 5120), BF16), ((192, 5120), BF16)],
        table, codes, delta_up, low2, high2, back, w_adj, coarse_pre, patch0, w_dns, fine_slope,
        cot_plane, ext0, ext0_edge,
    )
    total = total_over_devices(jnp.concatenate([grads_a, grads_b], axis=1))
    factor = 1.0 / math.sqrt(lax.axis_size(AXES) * 4 * 512)
    outs = call(
        lambda *refs: unfold(factor, *refs), "unfold",
        [(w_fine.shape, F32), (w_down.shape, F32), (w_coarse.shape, F32), (w_up.shape, F32)], [], total,
    )
    return (decoded[None], *outs)


def solution(mesh):
    in_specs = (
        P("rep", "space", None, None),
        P("rep", "space", None),
        P("rep", "space", None, None),
        P(),
        P(),
        P(),
        P(),
        P("rep", "space", None, None),
    )
    out_specs = (P("rep", "space", None, None), P(), P(), P(), P())
    return jax.shard_map(shards, mesh=mesh, in_specs=in_specs, out_specs=out_specs, check_vma=False)
```

```python
import math

import jax
import jax.numpy as jnp
import numpy as np
from jax import lax
from jax.experimental import pallas as pl
from jax.experimental.pallas import tpu as pltpu
from jax.sharding import Mesh
from jax.sharding import PartitionSpec as P

F32 = jnp.float32
BF16 = jnp.bfloat16
I32 = jnp.int32
CHIPS = ("z", "y", "x")
AXES = ("z", "y", "x", "core")
FINE_SHIFTS = [10 * (c - 1) + (e - 1) for c in range(3) for e in range(3)]
COARSE_SHIFTS = [6 * (c - 1) + (e - 1) for c in range(3) for e in range(3)]


def lane_tables():
    table = np.full((16, 2048), -1, np.int32)
    t = np.arange(128)
    y, z, inside = t // 10 - 1, t % 10 - 1, t < 100
    c, e = np.where(y < 0, 0, np.where(y >= 8, 2, 1)), np.where(z < 0, 0, np.where(z >= 8, 2, 1))
    table[0, :128] = np.where(inside, 3 * c + e, -1)
    table[1, :128] = np.where(inside, (y - 8 * (c - 1)) * 8 + (z - 8 * (e - 1)), 0)
    own = inside & (c == 1) & (e == 1)
    for b in range(4):
        table[4, 128 * b : 128 * b + 128] = np.where(own, 64 * b + y * 8 + z, -1)
    u = np.arange(64)
    cy, cz, cin = u // 6 - 1, u % 6 - 1, u < 36
    cc, ce = np.where(cy < 0, 0, np.where(cy >= 4, 2, 1)), np.where(cz < 0, 0, np.where(cz >= 4, 2, 1))
    for b in range(2):
        at = slice(64 * b, 64 * b + 64)
        table[2, at] = np.where(cin, 3 * cc + ce, -1)
        table[3, at] = np.where(cin, 6 * (cy - 4 * (cc - 1) + 1) + cz - 4 * (ce - 1) + 1, 0)
    cown = cin & (cc == 1) & (ce == 1)
    w = np.arange(64)
    for j in range(2):
        for l in range(2):
            for b in range(2):
                at = (2 * j + l) * 128 + 64 * b
                rows = 128 * b + 10 * (2 * cy + j + 1) + 2 * cz + l + 1
                table[5, at : at + 64] = np.where(cown, rows, -1)
            for b in range(4):
                ny, nz = w // 8, w % 8
                hit = (ny % 2 == j) & (nz % 2 == l)
                at = (2 * j + l) * 256 + 64 * b
                table[7, at : at + 64] = np.where(hit, 64 * b + 6 * (ny // 2 + 1) + nz // 2 + 1, -1)
                hit = own & (y % 2 == j) & (z % 2 == l)
                at = (2 * j + l) * 512 + 128 * b
                table[8, at : at + 128] = np.where(hit, 64 * b + 6 * (y // 2 + 1) + z // 2 + 1, -1)
    for b in range(2):
        table[6, 64 * b : 64 * b + 64] = 128 * b + 10 * (w // 8 + 1) + w % 8 + 1
    return table


TABLE = lane_tables()


def mm(a, b):
    return jnp.dot(a, b, preferred_element_type=F32)


def nt(a, b):
    return lax.dot_general(a, b, (((1,), (1,)), ((), ())), preferred_element_type=F32)


def roll(v, shift):
    return pltpu.roll(v, shift % 128, 1)


def onehot(code, rows):
    hit = lax.broadcasted_iota(I32, (rows, code.shape[1]), 0) == code
    return jnp.where(hit, 1.0, 0.0).astype(BF16)


def low_half(shape):
    return lax.broadcasted_iota(I32, shape, 1) < 64


def merge(low, first, second):
    return jnp.where(low, first, roll(second, 64))


def merge_high(low, first, second):
    return jnp.where(low, roll(first, 64), second)


def sigmoid(v):
    return 1.0 / (1.0 + jnp.exp(-v))


def silu(v):
    return v / (1.0 + jnp.exp(-v))


def slope(v):
    s = sigmoid(v)
    return s * (1.0 + v * (1.0 - s))


def raw_slots(neighbours, a, block, direction):
    found = jnp.full(direction.shape, -1, I32)
    for j in range(9):
        k = 9 * a + j
        entry = block if k == 13 else neighbours[block, k - (k > 13)]
        found = jnp.where(direction == j, entry, found)
    return found


def local_code(slots, cells):
    return jnp.where(slots >= 0, slots * 64 + cells, -1)


def edge_code(slots, cells, base, remote_slots):
    code = jnp.where((slots >= 0) & (slots < 4), slots * 64 + cells, -1)
    reach = (slots >= base) & (slots < base + 16)
    for j in range(4):
        hit = reach & (slots - base == remote_slots[j : j + 1])
        code = jnp.where(hit, 256 + j * 64 + cells, code)
    return code


def fine_slots(neighbours, table, a):
    direction = table[0:1, :128]
    return [raw_slots(neighbours, a, b, direction) for b in range(4)]


def coarse_slots(neighbours, table, a):
    direction = table[2:3, :128]
    low = low_half((1, 128))
    per_block = [raw_slots(neighbours, a, b, direction) for b in range(4)]
    return [jnp.where(low, per_block[0], per_block[1]), jnp.where(low, per_block[2], per_block[3])]


def arrived_slots(payload):
    return payload[128:144, :].astype(F32).astype(I32)


def tap_rows(w_ref):
    return jnp.concatenate([w_ref[:, 576 * a : 576 * a + 576] for a in range(3)], axis=0)


def put_taps(dst, at, plane, shifts):
    for s in range(plane.shape[1] // 128):
        piece = plane[:, 128 * s : 128 * s + 128]
        for j, shift in enumerate(shifts):
            moved = piece if shift == 0 else roll(piece, -shift)
            dst[64 * j : 64 * j + 64, at + 128 * s : at + 128 * s + 128] = moved


def natural_planes(ref):
    low = low_half((64, 128))
    planes = []
    for t in range(4):
        tiles = [ref[b, :, 128 * t : 128 * t + 128] for b in range(4)]
        planes.append(jnp.concatenate([merge(low, tiles[2 * p], tiles[2 * p + 1]) for p in range(2)], axis=1))
        planes.append(jnp.concatenate([merge_high(low, tiles[2 * p], tiles[2 * p + 1]) for p in range(2)], axis=1))
    return planes


def transposed_blocks(w, order):
    wt = w.astype(F32).T
    return jnp.concatenate([wt[64 * k : 64 * k + 64, :] for k in order], axis=1).astype(BF16)


def pack_faces(sends, low_tile, high_tile, to_upper, to_lower):
    low = low_half((64, 128))
    for p in range(2):
        to_upper[64 * p : 64 * p + 64, :] = merge_high(low, high_tile[2 * p], high_tile[2 * p + 1])
        to_lower[64 * p : 64 * p + 64, :] = merge(low, low_tile[2 * p], low_tile[2 * p + 1])
    rows = lax.broadcasted_iota(I32, (16, 128), 0)
    for side, out in ((0, to_upper), (1, to_lower)):
        slots = jnp.full((16, 128), -1, I32)
        for j in range(4):
            slot = jnp.int32(-1)
            for s in range(16):
                slot = jnp.where(sends[side, s] == j, s, slot)
            slots = jnp.where(rows == j, slot, slots)
        out[128:144, :] = slots.astype(F32).astype(BF16)


def fine_inner(neighbours, table, w_fine, w_down, w_coarse, w_up, feat, cot,
               pre, edges, up_back, ext, cot_plane, cot_patch, w_adj, w_ups, w_dns, taps):
    planes = natural_planes(feat)
    edges[0], edges[1] = planes[0], planes[7]
    cells = table[1:2, :128]
    code = jnp.concatenate([local_code(v, cells) for v in fine_slots(neighbours, table, 1)], axis=1)
    whole = mm(jnp.concatenate(planes, axis=0), onehot(code, 256)).astype(BF16)
    weight = tap_rows(w_fine)
    for x in range(8):
        plane = whole[64 * x : 64 * x + 64]
        ext[x] = plane
        put_taps(taps, 512 * x, plane, FINE_SHIFTS)
    for x in range(8):
        part = mm(weight, taps[:, 512 * x : 512 * x + 512])
        for a in range(3):
            out = x + 1 - a
            if 0 <= out < 8:
                piece = part[64 * a : 64 * a + 64]
                if x == max(out - 1, 0):
                    pre[out] = piece
                else:
                    pre[out] += piece
    placed = mm(jnp.concatenate(natural_planes(cot), axis=0), onehot(table[4:5, :512], 256)).astype(BF16)
    for x in range(8):
        cot_plane[x] = placed[64 * x : 64 * x + 64]
    down = onehot(table[5:6, :512], 256)
    for p in range(2):
        put_patches(cot_patch, mm(placed[:, 256 * p : 256 * p + 256], down).astype(BF16), p)
    up_back[...] = mm(w_up[...], cot_patch[...])
    for a in range(3):
        order = [(2 - a) * 9 + 8 - j for j in range(9)]
        w_adj[64 * a : 64 * a + 64, :] = transposed_blocks(w_coarse[...], order)
    for i in range(2):
        w_ups[64 * i : 64 * i + 64, :] = transposed_blocks(w_up[...], range(4 * i, 4 * i + 4))
        w_dns[64 * i : 64 * i + 64, :] = transposed_blocks(w_down[...], range(4 * i, 4 * i + 4))


def put_patches(dst, selected, pair):
    for x in range(8):
        for jl in range(4):
            at = ((x % 2) * 4 + jl) * 64
            lane = (x // 2) * 256 + pair * 128
            dst[at : at + 64, lane : lane + 128] = selected[64 * x : 64 * x + 64, 128 * jl : 128 * jl + 128]


def fine_outer(neighbours, table, from_lower, from_upper, edges, pre, w_fine, w_down,
               hidden, patch, coarse_pre, hidden1, pre_edge, ext_edge, to_upper, to_lower, taps):
    cells = table[1:2, :128]
    weight = tap_rows(w_fine)
    for side, a, base, payload in ((0, 0, 4, from_lower), (1, 2, 20, from_upper)):
        slots = arrived_slots(payload)
        code = jnp.concatenate([edge_code(v, cells, base, slots) for v in fine_slots(neighbours, table, a)], axis=1)
        pool = jnp.concatenate([edges[1 - side], payload[0:64, :], payload[64:128, :]], axis=1)
        plane = mm(pool, onehot(code, 512)).astype(BF16)
        ext_edge[side] = plane
        put_taps(taps, 512 * side, plane, FINE_SHIFTS)
        part = mm(weight[64 * a : 64 * a + 64], taps[:, 512 * side : 512 * side + 512])
        pre_edge[side] = pre[7 * side] + part
    for x in range(8):
        value = pre_edge[0] if x == 0 else pre_edge[1] if x == 7 else pre[x]
        hidden[x] = silu(value).astype(BF16)
    down = onehot(table[5:6, :512], 256)
    for p in range(2):
        rows = jnp.concatenate([hidden[x, :, 256 * p : 256 * p + 256] for x in range(8)], axis=0)
        put_patches(patch, mm(rows, down).astype(BF16), p)
    value = mm(w_down[...], patch[...])
    coarse_pre[...] = value
    value = silu(value).astype(BF16)
    hidden1[...] = value
    to_upper[...], to_lower[...] = value[:, 768:], value[:, :256]


def by_rows(v):
    return jnp.concatenate([v[:, 256 * x : 256 * x + 256] for x in range(4)], axis=0)


def coarse_inner_conv(field, select, weight, taps, ext):
    whole = mm(by_rows(field), select).astype(BF16)
    for x in range(4):
        plane = whole[64 * x : 64 * x + 64]
        if ext is not None:
            ext[:, 256 * x : 256 * x + 256] = plane
        put_taps(taps, 256 * x, plane, COARSE_SHIFTS)
    part = mm(weight, taps[:, :1024])
    sums = []
    for x in range(4):
        total = part[64:128, 256 * x : 256 * x + 256]
        if x > 0:
            total = total + part[0:64, 256 * x - 256 : 256 * x]
        if x < 3:
            total = total + part[128:192, 256 * x + 256 : 256 * x + 512]
        sums.append(total)
    return jnp.concatenate(sums, axis=1)


def coarse_outer_conv(codes, side, own_plane, arrived, weight, taps, at):
    pool = jnp.concatenate([own_plane, arrived], axis=1)
    plane = mm(pool, onehot(codes[side : side + 1, :], 512)).astype(BF16)
    put_taps(taps, at, plane, COARSE_SHIFTS)
    return mm(weight[128 * side : 128 * side + 64], taps[:, at : at + 256]), plane


def coarse_inner(neighbours, table, from_lower, from_upper, hidden1, pre, pre_edge, w_coarse, coarse_pre,
                 codes, ext, conv, fine_slope, coarse_slope, taps):
    coarse_slope[...] = slope(coarse_pre[...])
    cells = table[3:4, :128]
    for row, a, base, payload in ((0, 0, 4, from_lower), (1, 2, 20, from_upper)):
        slots = arrived_slots(payload)
        code = [edge_code(v, cells, base, slots) for v in coarse_slots(neighbours, table, a)]
        codes[row : row + 1, :] = jnp.concatenate(code, axis=1)
    code = [local_code(v, cells) for v in coarse_slots(neighbours, table, 1)]
    codes[2:3, :] = jnp.concatenate(code, axis=1)
    codes[3:8, :] = jnp.full((5, 256), -1, I32)
    select = onehot(codes[2:3, :], 256)
    conv[...] = coarse_inner_conv(hidden1[...], select, tap_rows(w_coarse), taps, ext)
    for x in range(8):
        value = pre_edge[0] if x == 0 else pre_edge[1] if x == 7 else pre[x]
        fine_slope[x] = slope(value)


def coarse_outer(codes, hidden1, from_lower, from_upper, conv, up_back, w_coarse,
                 gated, delta, ext_edge, to_upper, to_lower, taps):
    weight = tap_rows(w_coarse)
    low, ext_edge[0] = coarse_outer_conv(codes, 0, hidden1[:, 768:], from_lower[...], weight, taps, 0)
    high, ext_edge[1] = coarse_outer_conv(codes, 1, hidden1[:, :256], from_upper[...], weight, taps, 256)
    value = conv[...]
    value = jnp.concatenate([value[:, :256] + low, value[:, 256:768], value[:, 768:] + high], axis=1)
    gated[...] = silu(value).astype(BF16)
    value = (up_back[...] * slope(value)).astype(BF16)
    delta[...] = value
    to_upper[...], to_lower[...] = value[:, 768:], value[:, :256]


def decode(table, codes, gated, delta, ext, ext_edge, hidden, cot_patch, w_ups, w_adj,
           decoded, grads, back, taps, stack, spread):
    select = onehot(codes[2:3, :], 256)
    back[...] = coarse_inner_conv(delta[...], select, w_adj[...], taps, None)
    chosen = mm(by_rows(gated[...]), onehot(table[7:8, :1024], 256)).astype(BF16)
    for x in range(4):
        for jl in range(4):
            spread[64 * jl : 64 * jl + 64, 256 * x : 256 * x + 256] = (
                chosen[64 * x : 64 * x + 64, 256 * jl : 256 * jl + 256]
            )
    up = mm(w_ups[...], spread[...])
    compress = onehot(table[6:7, :128], 256)
    low = low_half((64, 128))
    for p in range(2):
        rows = jnp.concatenate([hidden[x, :, 256 * p : 256 * p + 256] for x in range(8)], axis=0)
        own = mm(rows, compress)
        for t in range(4):
            even, odd = [
                own[64 * x : 64 * x + 64] + up[64 * i : 64 * i + 64, 256 * t + 128 * p : 256 * t + 128 * p + 128]
                for i, x in ((0, 2 * t), (1, 2 * t + 1))
            ]
            decoded[2 * p, :, 128 * t : 128 * t + 128] = merge(low, even, odd).astype(BF16)
            decoded[2 * p + 1, :, 128 * t : 128 * t + 128] = merge_high(low, even, odd).astype(BF16)
    put_taps(taps, 0, ext_edge[0], COARSE_SHIFTS)
    for x in range(4):
        put_taps(taps, 256 + 256 * x, ext[:, 256 * x : 256 * x + 256], COARSE_SHIFTS)
    put_taps(taps, 1280, ext_edge[1], COARSE_SHIFTS)
    stack[...] = jnp.zeros(stack.shape, BF16)
    for a in range(3):
        stack[64 * a : 64 * a + 64, 256 * a : 256 * a + 1024] = delta[...]
    of_coarse = nt(taps[...], stack[...])
    of_up = jnp.concatenate([nt(cot_patch[...], gated[...]), jnp.zeros((64, 64), F32)], axis=0)
    put_grads(grads, of_coarse, of_up)


def finish(ready, table, codes, delta, from_lower, from_upper, back, w_adj, coarse_slope, patch, w_dns, fine_slope,
           cot_plane, ext, ext_edge, grads, coarse_taps, spread, taps, stack):
    ready[0]()
    weight = w_adj[...]
    low, _ = coarse_outer_conv(codes, 0, delta[:, 768:], from_lower[...], weight, coarse_taps, 0)
    high, _ = coarse_outer_conv(codes, 1, delta[:, :256], from_upper[...], weight, coarse_taps, 256)
    value = back[...]
    value = jnp.concatenate([value[:, :256] + low, value[:, 256:768], value[:, 768:] + high], axis=1)
    ready[1]()
    down = (value * coarse_slope[...]).astype(BF16)
    ready[2]()
    of_down = jnp.concatenate([nt(patch[...], down), jnp.zeros((64, 64), F32)], axis=0)
    chosen = mm(by_rows(down), onehot(table[8:9, :2048], 256)).astype(BF16)
    for x in range(4):
        for jl in range(4):
            spread[64 * jl : 64 * jl + 64, 512 * x : 512 * x + 512] = (
                chosen[64 * x : 64 * x + 64, 512 * jl : 512 * jl + 512]
            )
    for a in range(3):
        for plane in range(10):
            if not 0 <= plane - a < 8:
                stack[64 * a : 64 * a + 64, 512 * plane : 512 * plane + 512] = jnp.zeros((64, 512), BF16)
    for wait in ready[3:]:
        wait()
    for half in range(4):
        raised = mm(w_dns[...], spread[:, 512 * half : 512 * half + 512])
        for i in range(2):
            x = 2 * half + i
            total = cot_plane[x].astype(F32) + raised[64 * i : 64 * i + 64]
            fine = (total * fine_slope[x]).astype(BF16)
            for a in range(3):
                at = 512 * (x + a)
                stack[64 * a : 64 * a + 64, at : at + 512] = fine
    put_taps(taps, 0, ext_edge[0], FINE_SHIFTS)
    for x in range(8):
        put_taps(taps, 512 * x + 512, ext[x], FINE_SHIFTS)
    put_taps(taps, 4608, ext_edge[1], FINE_SHIFTS)
    put_grads(grads, nt(taps[...], stack[...]), of_down)


def put_grads(grads, wide, narrow):
    grads[0:576, :] = wide[:, :128]
    grads[576:1152, :] = jnp.concatenate([wide[:, 128:], narrow], axis=1)


def unfold(factor, total, grad_fine, grad_down, grad_coarse, grad_up):
    for at, wide, narrow in ((0, grad_fine, grad_down), (1152, grad_coarse, grad_up)):
        both = jnp.concatenate([total[at : at + 576, :], total[at + 576 : at + 1152, :]], axis=1)
        turned = (both.astype(F32) * factor).T
        wide[...] = jnp.concatenate([turned[64 * a : 64 * a + 64, :] for a in range(3)], axis=1)
        narrow[...] = turned[192:256, :512]


GRANT = 53 * 1024 * 1024
VMEM_SPEC = pl.BlockSpec(memory_space=pltpu.VMEM)
SMEM_SPEC = pl.BlockSpec(memory_space=pltpu.SMEM)
HBM_SPEC = pl.BlockSpec(memory_space=pltpu.HBM)


def whole(shape):
    return pl.BlockSpec(shape, lambda i: (0,) * len(shape))


def place(shape, kind):
    size = math.prod(shape) * jnp.dtype(kind).itemsize
    return VMEM_SPEC if size <= 64 * 1024 or shape == (1152, 128) else whole(shape)


def call(kernel, name, outs, scratch, near, far=(), late=False):
    counts = (len(near), len(far), len(outs), len(scratch), len(far))
    far_outs = [k for k, (away, _, _) in enumerate(outs) if away]

    def body(*refs):
        groups, at = [], 0
        for count in counts:
            groups.append(refs[at : at + count])
            at += count
        near_refs, far_refs, out_refs, own, landed = groups
        staged, (in_sem, out_sem) = refs[at : at + len(far_outs)], refs[at + len(far_outs) :]
        arriving = [pltpu.make_async_copy(s, d, in_sem.at[k]) for k, (s, d) in enumerate(zip(far_refs, landed))]
        for copy in arriving:
            copy.start()
        results = list(out_refs)
        for k, buffer in zip(far_outs, staged):
            results[k] = buffer
        if late:
            kernel([copy.wait for copy in arriving], *near_refs, *landed, *results, *own)
        else:
            for copy in arriving:
                copy.wait()
            kernel(*near_refs, *landed, *results, *own)
        leaving = [
            pltpu.make_async_copy(buffer, out_refs[k], out_sem.at[n])
            for n, (k, buffer) in enumerate(zip(far_outs, staged))
        ]
        for copy in leaving:
            copy.start()
        for copy in leaving:
            copy.wait()

    small = ((4, 26), (2, 16))
    return pl.pallas_call(
        body,
        name=name,
        out_shape=[jax.ShapeDtypeStruct(shape, kind) for _, shape, kind in outs],
        grid=(1,),
        in_specs=[SMEM_SPEC if x.shape in small else place(x.shape, x.dtype) for x in near] + [HBM_SPEC] * len(far),
        out_specs=[HBM_SPEC if away else place(shape, kind) for away, shape, kind in outs],
        scratch_shapes=[pltpu.VMEM(shape, kind) for shape, kind in scratch]
        + [pltpu.VMEM(x.shape, x.dtype) for x in far]
        + [pltpu.VMEM(outs[k][1], outs[k][2]) for k in far_outs]
        + [pltpu.SemaphoreType.DMA((max(len(far), 1),)), pltpu.SemaphoreType.DMA((max(len(far_outs), 1),))],
        compiler_params=pltpu.CompilerParams(vmem_limit_bytes=GRANT),
    )(*near, *far)


def passed_along(block, distance):
    devices = range(lax.axis_size(CHIPS))
    route = [(i - distance, i) for i in devices if i - distance in devices]
    return lax.ppermute(block, CHIPS, route)


def other_core(x):
    return lax.ppermute(x, "core", [(0, 1), (1, 0)])


def dealt(x, axes):
    count = lax.axis_size(axes)
    return lax.all_to_all(x.reshape(count, -1, 128), axes, 0, 0, tiled=True)


def told(x, axes):
    return dealt(jnp.broadcast_to(x, (lax.axis_size(axes), *x.shape)), axes)


def summed(blocks):
    total = blocks[0].astype(F32)
    for k in range(1, blocks.shape[0]):
        total = total + blocks[k].astype(F32)
    return total


def total_over_devices(x):
    core = lax.axis_index("core")
    half = x.shape[0] // 2
    keep = lax.dynamic_slice_in_dim(x, core * half, half, 0)
    send = lax.dynamic_slice_in_dim(x, (1 - core) * half, half, 0)
    x = keep + other_core(send.astype(BF16)).astype(F32)
    x = summed(dealt(x.astype(BF16), ("y", "x")))
    x = summed(told(x.astype(BF16), "z"))
    x = told(x.astype(BF16), ("y", "x")).reshape(half, 128)
    other = other_core(x)
    return jnp.concatenate([jnp.where(core == 0, x, other), jnp.where(core == 0, other, x)], axis=0)


def shards(features, neighbours, send_list, w_fine, w_down, w_coarse, w_up, cotangent):
    feat, cot = features[0], cotangent[0]
    near, sends = neighbours[0], send_list[0, 0]
    table = jnp.asarray(TABLE)
    tile = (4, 64, 128)
    face = jax.ShapeDtypeStruct((144, 128), BF16)
    to_upper, to_lower = pl.pallas_call(
        pack_faces,
        name="pack_faces",
        grid=(1,),
        out_shape=[face, face],
        in_specs=[SMEM_SPEC, pl.BlockSpec(tile, lambda i: (0, 0, 0)), pl.BlockSpec(tile, lambda i: (0, 0, 3))],
        out_specs=[pl.BlockSpec((144, 128), lambda i: (0, 0))] * 2,
        compiler_params=pltpu.CompilerParams(vmem_limit_bytes=60 * 1024 * 1024),
    )(sends, feat, feat)
    from_lower, from_upper = passed_along(to_upper, 1), passed_along(to_lower, -1)

    fine = (8, 64, 512)
    pre, edges, up_back, ext0, cot_plane, cot_patch, w_adj, w_ups, w_dns = call(
        fine_inner, "fine_inner",
        [(0, fine, F32), (0, (2, 64, 256), BF16), (0, (64, 1024), F32), (0, fine, BF16), (0, fine, BF16),
         (0, (512, 1024), BF16), (0, (192, 576), BF16), (0, (128, 256), BF16), (0, (128, 256), BF16)],
        [((576, 4096), BF16)],
        [near, table, w_fine, w_down, w_coarse], [w_up, feat, cot],
    )
    hidden0, patch0, coarse_pre, hidden1, pre_edge, ext0_edge, to_upper, to_lower = call(
        fine_outer, "fine_outer",
        [(0, fine, BF16), (0, (512, 1024), BF16), (0, (64, 1024), F32), (0, (64, 1024), BF16), (0, (2, 64, 512), F32),
         (0, (2, 64, 512), BF16), (0, (64, 256), BF16), (0, (64, 256), BF16)],
        [((576, 1024), BF16)],
        [near, table, from_lower, from_upper, edges, pre, w_fine, w_down],
    )
    low1, high1 = passed_along(to_upper, 1), passed_along(to_lower, -1)
    codes, ext1, conv, fine_slope, coarse_slope = call(
        coarse_inner, "coarse_inner",
        [(0, (8, 256), I32), (0, (64, 1024), BF16), (0, (64, 1024), F32), (0, fine, F32), (0, (64, 1024), F32)],
        [((576, 1024), BF16)],
        [near, table, from_lower, from_upper, hidden1, pre, pre_edge, w_coarse, coarse_pre],
    )
    gated, delta_up, ext1_edge, to_upper, to_lower = call(
        coarse_outer, "coarse_outer",
        [(0, (64, 1024), BF16), (0, (64, 1024), BF16), (0, (2, 64, 256), BF16), (0, (64, 256), BF16), (0, (64, 256), BF16)],
        [((576, 512), BF16)],
        [codes, hidden1, low1, high1, conv, up_back, w_coarse],
    )
    low2, high2 = passed_along(to_upper, 1), passed_along(to_lower, -1)
    decoded, grads_b, back = call(
        decode, "decode",
        [(0, (4, 64, 512), BF16), (0, (1152, 128), F32), (0, (64, 1024), F32)],
        [((576, 1536), BF16), ((192, 1536), BF16), ((256, 1024), BF16)],
        [table, codes, gated, delta_up, ext1, ext1_edge], [hidden0, cot_patch, w_ups, w_adj],
    )
    (grads_a,) = call(
        finish, "finish",
        [(0, (1152, 128), F32)],
        [((576, 512), BF16), ((256, 2048), BF16), ((576, 5120), BF16), ((192, 5120), BF16)],
        [table, codes, delta_up, low2, high2, back],
        [w_adj, coarse_slope, patch0, w_dns, fine_slope, cot_plane, ext0, ext0_edge], late=True,
    )
    total = total_over_devices(jnp.concatenate([grads_a, grads_b], axis=0))
    factor = 1.0 / math.sqrt(lax.axis_size(AXES) * 4 * 512)
    outs = call(
        lambda *refs: unfold(factor, *refs), "unfold",
        [(0, w_fine.shape, F32), (0, w_down.shape, F32), (0, w_coarse.shape, F32), (0, w_up.shape, F32)], [], [total],
    )
    return (decoded[None], *outs)


def solution(mesh):
    chips = mesh.devices.shape[0]
    x = min(4, chips)
    y = min(4, chips // x)
    grid = Mesh(mesh.devices.reshape(chips // (x * y), y, x, -1), AXES)
    in_specs = (
        P("core", CHIPS, None, None),
        P("core", CHIPS, None),
        P("core", CHIPS, None, None),
        P(),
        P(),
        P(),
        P(),
        P("core", CHIPS, None, None),
    )
    out_specs = (P("core", CHIPS, None, None), P(), P(), P(), P())
    return jax.shard_map(shards, mesh=grid, in_specs=in_specs, out_specs=out_specs, check_vma=False)
```

```python
import math

import jax
import jax.numpy as jnp
import numpy as np
from jax import lax
from jax.experimental import pallas as pl
from jax.experimental.pallas import tpu as pltpu
from jax.sharding import Mesh
from jax.sharding import PartitionSpec as P

F32 = jnp.float32
BF16 = jnp.bfloat16
I32 = jnp.int32
CHIPS = ("z", "y", "x")
AXES = ("z", "y", "x", "core")
FINE_SHIFTS = [10 * (c - 1) + (e - 1) for c in range(3) for e in range(3)]
COARSE_SHIFTS = [6 * (c - 1) + (e - 1) for c in range(3) for e in range(3)]


def lane_tables():
    table = np.full((16, 2048), -1, np.int32)
    t = np.arange(128)
    y, z, inside = t // 10 - 1, t % 10 - 1, t < 100
    c, e = np.where(y < 0, 0, np.where(y >= 8, 2, 1)), np.where(z < 0, 0, np.where(z >= 8, 2, 1))
    table[0, :128] = np.where(inside, 3 * c + e, -1)
    table[1, :128] = np.where(inside, (y - 8 * (c - 1)) * 8 + (z - 8 * (e - 1)), 0)
    own = inside & (c == 1) & (e == 1)
    for b in range(4):
        table[4, 128 * b : 128 * b + 128] = np.where(own, 64 * b + y * 8 + z, -1)
    u = np.arange(64)
    cy, cz, cin = u // 6 - 1, u % 6 - 1, u < 36
    cc, ce = np.where(cy < 0, 0, np.where(cy >= 4, 2, 1)), np.where(cz < 0, 0, np.where(cz >= 4, 2, 1))
    for b in range(2):
        at = slice(64 * b, 64 * b + 64)
        table[2, at] = np.where(cin, 3 * cc + ce, -1)
        table[3, at] = np.where(cin, 6 * (cy - 4 * (cc - 1) + 1) + cz - 4 * (ce - 1) + 1, 0)
    cown = cin & (cc == 1) & (ce == 1)
    w = np.arange(64)
    for j in range(2):
        for l in range(2):
            for b in range(2):
                at = (2 * j + l) * 128 + 64 * b
                rows = 128 * b + 10 * (2 * cy + j + 1) + 2 * cz + l + 1
                table[5, at : at + 64] = np.where(cown, rows, -1)
            for b in range(4):
                ny, nz = w // 8, w % 8
                hit = (ny % 2 == j) & (nz % 2 == l)
                at = (2 * j + l) * 256 + 64 * b
                table[7, at : at + 64] = np.where(hit, 64 * b + 6 * (ny // 2 + 1) + nz // 2 + 1, -1)
                hit = own & (y % 2 == j) & (z % 2 == l)
                at = (2 * j + l) * 512 + 128 * b
                table[8, at : at + 128] = np.where(hit, 64 * b + 6 * (y // 2 + 1) + z // 2 + 1, -1)
    for b in range(2):
        table[6, 64 * b : 64 * b + 64] = 128 * b + 10 * (w // 8 + 1) + w % 8 + 1
    return table


TABLE = lane_tables()


def mm(a, b):
    return jnp.dot(a, b, preferred_element_type=F32)


def nt(a, b):
    return lax.dot_general(a, b, (((1,), (1,)), ((), ())), preferred_element_type=F32)


def roll(v, shift):
    return pltpu.roll(v, shift % 128, 1)


def onehot(code, rows):
    hit = lax.broadcasted_iota(I32, (rows, code.shape[1]), 0) == code
    return jnp.where(hit, 1.0, 0.0).astype(BF16)


def low_half(shape):
    return lax.broadcasted_iota(I32, shape, 1) < 64


def merge(low, first, second):
    return jnp.where(low, first, roll(second, 64))


def merge_high(low, first, second):
    return jnp.where(low, roll(first, 64), second)


def sigmoid(v):
    return 1.0 / (1.0 + jnp.exp(-v))


def silu(v):
    return v / (1.0 + jnp.exp(-v))


def slope(v):
    s = sigmoid(v)
    return s * (1.0 + v * (1.0 - s))


def raw_slots(neighbours, a, block, direction):
    found = jnp.full(direction.shape, -1, I32)
    for j in range(9):
        k = 9 * a + j
        entry = block if k == 13 else neighbours[block, k - (k > 13)]
        found = jnp.where(direction == j, entry, found)
    return found


def local_code(slots, cells):
    return jnp.where(slots >= 0, slots * 64 + cells, -1)


def edge_code(slots, cells, base, remote_slots):
    code = jnp.where((slots >= 0) & (slots < 4), slots * 64 + cells, -1)
    reach = (slots >= base) & (slots < base + 16)
    for j in range(4):
        hit = reach & (slots - base == remote_slots[j : j + 1])
        code = jnp.where(hit, 256 + j * 64 + cells, code)
    return code


def fine_slots(neighbours, table, a):
    direction = table[0:1, :128]
    return [raw_slots(neighbours, a, b, direction) for b in range(4)]


def coarse_slots(neighbours, table, a):
    direction = table[2:3, :128]
    low = low_half((1, 128))
    per_block = [raw_slots(neighbours, a, b, direction) for b in range(4)]
    return [jnp.where(low, per_block[0], per_block[1]), jnp.where(low, per_block[2], per_block[3])]


def arrived_slots(payload):
    return payload[128:144, :].astype(F32).astype(I32)


def tap_rows(w_ref):
    return jnp.concatenate([w_ref[:, 576 * a : 576 * a + 576] for a in range(3)], axis=0)


def put_taps(dst, at, plane, shifts):
    for s in range(plane.shape[1] // 128):
        piece = plane[:, 128 * s : 128 * s + 128]
        for j, shift in enumerate(shifts):
            moved = piece if shift == 0 else roll(piece, -shift)
            dst[64 * j : 64 * j + 64, at + 128 * s : at + 128 * s + 128] = moved


def natural_planes(ref):
    low = low_half((64, 128))
    planes = []
    for t in range(4):
        tiles = [ref[b, :, 128 * t : 128 * t + 128] for b in range(4)]
        planes.append(jnp.concatenate([merge(low, tiles[2 * p], tiles[2 * p + 1]) for p in range(2)], axis=1))
        planes.append(jnp.concatenate([merge_high(low, tiles[2 * p], tiles[2 * p + 1]) for p in range(2)], axis=1))
    return planes


def transposed_blocks(w, order):
    wt = w.astype(F32).T
    return jnp.concatenate([wt[64 * k : 64 * k + 64, :] for k in order], axis=1).astype(BF16)


def pack_faces(core, sends, low_tile, high_tile, to_upper, to_lower):
    low = low_half((64, 128))
    for p in range(2):
        to_upper[64 * p : 64 * p + 64, :] = merge_high(low, high_tile[2 * p], high_tile[2 * p + 1])
        to_lower[64 * p : 64 * p + 64, :] = merge(low, low_tile[2 * p], low_tile[2 * p + 1])
    rows = lax.broadcasted_iota(I32, (16, 128), 0)
    for side, out in ((0, to_upper), (1, to_lower)):
        slots = jnp.full((16, 128), -1, I32)
        for j in range(4):
            slot = jnp.int32(-1)
            for s in range(16):
                slot = jnp.where(sends[side, s] == j, s, slot)
            slots = jnp.where(rows == j, slot, slots)
        out[128:144, :] = slots.astype(F32).astype(BF16)


def fine_inner(neighbours, table, w_fine, w_down, w_coarse, w_up, feat, cot,
               pre, edges, up_back, ext, cot_plane, cot_patch, w_adj, w_ups, w_dns, taps):
    planes = natural_planes(feat)
    edges[0], edges[1] = planes[0], planes[7]
    cells = table[1:2, :128]
    code = jnp.concatenate([local_code(v, cells) for v in fine_slots(neighbours, table, 1)], axis=1)
    whole = mm(jnp.concatenate(planes, axis=0), onehot(code, 256)).astype(BF16)
    weight = tap_rows(w_fine)
    for x in range(8):
        plane = whole[64 * x : 64 * x + 64]
        ext[x] = plane
        put_taps(taps, 512 * x, plane, FINE_SHIFTS)
    for x in range(8):
        part = mm(weight, taps[:, 512 * x : 512 * x + 512])
        for a in range(3):
            out = x + 1 - a
            if 0 <= out < 8:
                piece = part[64 * a : 64 * a + 64]
                if x == max(out - 1, 0):
                    pre[out] = piece
                else:
                    pre[out] += piece
    placed = mm(jnp.concatenate(natural_planes(cot), axis=0), onehot(table[4:5, :512], 256)).astype(BF16)
    for x in range(8):
        cot_plane[x] = placed[64 * x : 64 * x + 64]
    down = onehot(table[5:6, :512], 256)
    for p in range(2):
        put_patches(cot_patch, mm(placed[:, 256 * p : 256 * p + 256], down).astype(BF16), p)
    up_back[...] = mm(w_up[...], cot_patch[...])
    for a in range(3):
        order = [(2 - a) * 9 + 8 - j for j in range(9)]
        w_adj[64 * a : 64 * a + 64, :] = transposed_blocks(w_coarse[...], order)
    for i in range(2):
        w_ups[64 * i : 64 * i + 64, :] = transposed_blocks(w_up[...], range(4 * i, 4 * i + 4))
        w_dns[64 * i : 64 * i + 64, :] = transposed_blocks(w_down[...], range(4 * i, 4 * i + 4))


def put_patches(dst, selected, pair):
    for x in range(8):
        for jl in range(4):
            at = ((x % 2) * 4 + jl) * 64
            lane = (x // 2) * 256 + pair * 128
            dst[at : at + 64, lane : lane + 128] = selected[64 * x : 64 * x + 64, 128 * jl : 128 * jl + 128]


def fine_outer(neighbours, table, from_lower, from_upper, edges, pre, w_fine, w_down,
               hidden, patch, coarse_pre, hidden1, pre_edge, ext_edge, to_upper, to_lower, taps):
    cells = table[1:2, :128]
    weight = tap_rows(w_fine)
    for side, a, base, payload in ((0, 0, 4, from_lower), (1, 2, 20, from_upper)):
        slots = arrived_slots(payload)
        code = jnp.concatenate([edge_code(v, cells, base, slots) for v in fine_slots(neighbours, table, a)], axis=1)
        pool = jnp.concatenate([edges[1 - side], payload[0:64, :], payload[64:128, :]], axis=1)
        plane = mm(pool, onehot(code, 512)).astype(BF16)
        ext_edge[side] = plane
        put_taps(taps, 512 * side, plane, FINE_SHIFTS)
        part = mm(weight[64 * a : 64 * a + 64], taps[:, 512 * side : 512 * side + 512])
        pre_edge[side] = pre[7 * side] + part
    for x in range(8):
        value = pre_edge[0] if x == 0 else pre_edge[1] if x == 7 else pre[x]
        hidden[x] = silu(value).astype(BF16)
    down = onehot(table[5:6, :512], 256)
    for p in range(2):
        rows = jnp.concatenate([hidden[x, :, 256 * p : 256 * p + 256] for x in range(8)], axis=0)
        put_patches(patch, mm(rows, down).astype(BF16), p)
    value = mm(w_down[...], patch[...])
    coarse_pre[...] = value
    value = silu(value).astype(BF16)
    hidden1[...] = value
    to_upper[...], to_lower[...] = value[:, 768:], value[:, :256]


def by_rows(v):
    return jnp.concatenate([v[:, 256 * x : 256 * x + 256] for x in range(4)], axis=0)


def coarse_inner_conv(field, select, weight, taps, ext):
    whole = mm(by_rows(field), select).astype(BF16)
    for x in range(4):
        plane = whole[64 * x : 64 * x + 64]
        if ext is not None:
            ext[:, 256 * x : 256 * x + 256] = plane
        put_taps(taps, 256 * x, plane, COARSE_SHIFTS)
    part = mm(weight, taps[:, :1024])
    sums = []
    for x in range(4):
        total = part[64:128, 256 * x : 256 * x + 256]
        if x > 0:
            total = total + part[0:64, 256 * x - 256 : 256 * x]
        if x < 3:
            total = total + part[128:192, 256 * x + 256 : 256 * x + 512]
        sums.append(total)
    return jnp.concatenate(sums, axis=1)


def coarse_outer_conv(codes, side, own_plane, arrived, weight, taps, at):
    pool = jnp.concatenate([own_plane, arrived], axis=1)
    plane = mm(pool, onehot(codes[side : side + 1, :], 512)).astype(BF16)
    put_taps(taps, at, plane, COARSE_SHIFTS)
    return mm(weight[128 * side : 128 * side + 64], taps[:, at : at + 256]), plane


def coarse_inner(neighbours, table, from_lower, from_upper, hidden1, pre, pre_edge, w_coarse, coarse_pre,
                 codes, ext, conv, fine_slope, coarse_slope, taps):
    coarse_slope[...] = slope(coarse_pre[...])
    cells = table[3:4, :128]
    for row, a, base, payload in ((0, 0, 4, from_lower), (1, 2, 20, from_upper)):
        slots = arrived_slots(payload)
        code = [edge_code(v, cells, base, slots) for v in coarse_slots(neighbours, table, a)]
        codes[row : row + 1, :] = jnp.concatenate(code, axis=1)
    code = [local_code(v, cells) for v in coarse_slots(neighbours, table, 1)]
    codes[2:3, :] = jnp.concatenate(code, axis=1)
    codes[3:8, :] = jnp.full((5, 256), -1, I32)
    select = onehot(codes[2:3, :], 256)
    conv[...] = coarse_inner_conv(hidden1[...], select, tap_rows(w_coarse), taps, ext)
    for x in range(8):
        value = pre_edge[0] if x == 0 else pre_edge[1] if x == 7 else pre[x]
        fine_slope[x] = slope(value)


def coarse_outer(codes, hidden1, from_lower, from_upper, conv, up_back, w_coarse,
                 gated, delta, ext_edge, to_upper, to_lower, taps):
    weight = tap_rows(w_coarse)
    low, ext_edge[0] = coarse_outer_conv(codes, 0, hidden1[:, 768:], from_lower[...], weight, taps, 0)
    high, ext_edge[1] = coarse_outer_conv(codes, 1, hidden1[:, :256], from_upper[...], weight, taps, 256)
    value = conv[...]
    value = jnp.concatenate([value[:, :256] + low, value[:, 256:768], value[:, 768:] + high], axis=1)
    gated[...] = silu(value).astype(BF16)
    value = (up_back[...] * slope(value)).astype(BF16)
    delta[...] = value
    to_upper[...], to_lower[...] = value[:, 768:], value[:, :256]


def decode(table, codes, gated, delta, ext, ext_edge, hidden, cot_patch, w_ups, w_adj,
           decoded, grads, back, taps, stack, spread):
    select = onehot(codes[2:3, :], 256)
    back[...] = coarse_inner_conv(delta[...], select, w_adj[...], taps, None)
    chosen = mm(by_rows(gated[...]), onehot(table[7:8, :1024], 256)).astype(BF16)
    for x in range(4):
        for jl in range(4):
            spread[64 * jl : 64 * jl + 64, 256 * x : 256 * x + 256] = (
                chosen[64 * x : 64 * x + 64, 256 * jl : 256 * jl + 256]
            )
    up = mm(w_ups[...], spread[...])
    compress = onehot(table[6:7, :128], 256)
    low = low_half((64, 128))
    for p in range(2):
        rows = jnp.concatenate([hidden[x, :, 256 * p : 256 * p + 256] for x in range(8)], axis=0)
        own = mm(rows, compress)
        for t in range(4):
            even, odd = [
                own[64 * x : 64 * x + 64] + up[64 * i : 64 * i + 64, 256 * t + 128 * p : 256 * t + 128 * p + 128]
                for i, x in ((0, 2 * t), (1, 2 * t + 1))
            ]
            decoded[2 * p, :, 128 * t : 128 * t + 128] = merge(low, even, odd).astype(BF16)
            decoded[2 * p + 1, :, 128 * t : 128 * t + 128] = merge_high(low, even, odd).astype(BF16)
    put_taps(taps, 0, ext_edge[0], COARSE_SHIFTS)
    for x in range(4):
        put_taps(taps, 256 + 256 * x, ext[:, 256 * x : 256 * x + 256], COARSE_SHIFTS)
    put_taps(taps, 1280, ext_edge[1], COARSE_SHIFTS)
    stack[...] = jnp.zeros(stack.shape, BF16)
    for a in range(3):
        stack[64 * a : 64 * a + 64, 256 * a : 256 * a + 1024] = delta[...]
    of_coarse = nt(taps[...], stack[...])
    of_up = jnp.concatenate([nt(cot_patch[...], gated[...]), jnp.zeros((64, 64), F32)], axis=0)
    put_grads(grads, of_coarse, of_up)


def finish(core, table, codes, delta, from_lower, from_upper, back, w_adj, coarse_slope, patch, w_dns, fine_slope,
           cot_plane, ext, ext_edge, grads_b, keep, send, coarse_taps, spread, taps, stack, grads):
    weight = w_adj[...]
    low, _ = coarse_outer_conv(codes, 0, delta[:, 768:], from_lower[...], weight, coarse_taps, 0)
    high, _ = coarse_outer_conv(codes, 1, delta[:, :256], from_upper[...], weight, coarse_taps, 256)
    value = back[...]
    value = jnp.concatenate([value[:, :256] + low, value[:, 256:768], value[:, 768:] + high], axis=1)
    down = (value * coarse_slope[...]).astype(BF16)
    of_down = jnp.concatenate([nt(patch[...], down), jnp.zeros((64, 64), F32)], axis=0)
    chosen = mm(by_rows(down), onehot(table[8:9, :2048], 256)).astype(BF16)
    for x in range(4):
        for jl in range(4):
            spread[64 * jl : 64 * jl + 64, 512 * x : 512 * x + 512] = (
                chosen[64 * x : 64 * x + 64, 512 * jl : 512 * jl + 512]
            )
    for a in range(3):
        for plane in range(10):
            if not 0 <= plane - a < 8:
                stack[64 * a : 64 * a + 64, 512 * plane : 512 * plane + 512] = jnp.zeros((64, 512), BF16)
    for half in range(4):
        raised = mm(w_dns[...], spread[:, 512 * half : 512 * half + 512])
        for i in range(2):
            x = 2 * half + i
            total = cot_plane[x].astype(F32) + raised[64 * i : 64 * i + 64]
            fine = (total * fine_slope[x]).astype(BF16)
            for a in range(3):
                at = 512 * (x + a)
                stack[64 * a : 64 * a + 64, at : at + 512] = fine
    put_taps(taps, 0, ext_edge[0], FINE_SHIFTS)
    for x in range(8):
        put_taps(taps, 512 * x + 512, ext[x], FINE_SHIFTS)
    put_taps(taps, 4608, ext_edge[1], FINE_SHIFTS)
    put_grads(grads, nt(taps[...], stack[...]), of_down)
    first = core[0] == 0

    @pl.when(first)
    def _():
        keep[...] = grads[...]
        send[...] = grads_b[...].astype(BF16)

    @pl.when(jnp.logical_not(first))
    def _():
        keep[...] = grads_b[...]
        send[...] = grads[...].astype(BF16)


def put_grads(grads, wide, narrow):
    grads[0:576, :] = wide[:, :128]
    grads[576:1152, :] = jnp.concatenate([wide[:, 128:], narrow], axis=1)


def unfold(factor, core, own, other, grad_fine, grad_down, grad_coarse, grad_up):
    def spell(half, wide, narrow):
        both = jnp.concatenate([half[0:576, :], half[576:1152, :]], axis=1)
        turned = (both.astype(F32) * factor).T
        wide[...] = jnp.concatenate([turned[64 * a : 64 * a + 64, :] for a in range(3)], axis=1)
        narrow[...] = turned[192:256, :512]

    first = core[0] == 0

    @pl.when(first)
    def _():
        spell(own, grad_fine, grad_down)
        spell(other, grad_coarse, grad_up)

    @pl.when(jnp.logical_not(first))
    def _():
        spell(other, grad_fine, grad_down)
        spell(own, grad_coarse, grad_up)


VMEM_SPEC = pl.BlockSpec(memory_space=pltpu.VMEM)
SMEM_SPEC = pl.BlockSpec(memory_space=pltpu.SMEM)
HBM_SPEC = pl.BlockSpec(memory_space=pltpu.HBM)


def call(kernel, name, megabytes, outs, scratch, near, far=(), late=False):
    counts = (len(near), len(far), len(outs), len(scratch), len(far))
    far_outs = [k for k, (away, _, _) in enumerate(outs) if away]

    def body(*refs):
        groups, at = [], 0
        for count in counts:
            groups.append(refs[at : at + count])
            at += count
        near_refs, far_refs, out_refs, own, landed = groups
        staged, (in_sem, out_sem) = refs[at : at + len(far_outs)], refs[at + len(far_outs) :]
        arriving = [pltpu.make_async_copy(s, d, in_sem.at[k]) for k, (s, d) in enumerate(zip(far_refs, landed))]
        for copy in arriving:
            copy.start()
        results = list(out_refs)
        for k, buffer in zip(far_outs, staged):
            results[k] = buffer
        if late:
            kernel([copy.wait for copy in arriving], *near_refs, *landed, *results, *own)
        else:
            for copy in arriving:
                copy.wait()
            kernel(*near_refs, *landed, *results, *own)
        leaving = [
            pltpu.make_async_copy(buffer, out_refs[k], out_sem.at[n])
            for n, (k, buffer) in enumerate(zip(far_outs, staged))
        ]
        for copy in leaving:
            copy.start()
        for copy in leaving:
            copy.wait()

    small = ((4, 26), (1,))
    return pl.pallas_call(
        body,
        name=name,
        out_shape=[jax.ShapeDtypeStruct(shape, kind) for _, shape, kind in outs],
        in_specs=[SMEM_SPEC if x.shape in small else VMEM_SPEC for x in near] + [HBM_SPEC] * len(far),
        out_specs=[HBM_SPEC if away else VMEM_SPEC for away, _, _ in outs],
        scratch_shapes=[pltpu.VMEM(shape, kind) for shape, kind in scratch]
        + [pltpu.VMEM(x.shape, x.dtype) for x in far]
        + [pltpu.VMEM(outs[k][1], outs[k][2]) for k in far_outs]
        + [pltpu.SemaphoreType.DMA((max(len(far), 1),)), pltpu.SemaphoreType.DMA((max(len(far_outs), 1),))],
        compiler_params=pltpu.CompilerParams(vmem_limit_bytes=megabytes * 1024 * 1024),
    )(*near, *far)


def passed_along(block, distance):
    devices = range(lax.axis_size(CHIPS))
    route = [(i - distance, i) for i in devices if i - distance in devices]
    return lax.ppermute(block, CHIPS, route)


def other_core(x):
    return lax.ppermute(x, "core", [(0, 1), (1, 0)])


def dealt(x, axes):
    count = lax.axis_size(axes)
    return lax.all_to_all(x.reshape(count, -1, 128), axes, 0, 0, tiled=True)


def told(x, axes):
    return dealt(jnp.broadcast_to(x, (lax.axis_size(axes), *x.shape)), axes)


def summed(blocks):
    total = blocks[0].astype(F32)
    for k in range(1, blocks.shape[0]):
        total = total + blocks[k].astype(F32)
    return total


def total_over_devices(keep, send):
    x = keep + other_core(send).astype(F32)
    x = summed(dealt(x.astype(BF16), ("y", "x")))
    x = summed(told(x.astype(BF16), "z"))
    return told(x.astype(BF16), ("y", "x")).reshape(keep.shape)


def shards(features, neighbours, send_list, w_fine, w_down, w_coarse, w_up, cotangent):
    feat, cot = features[0], cotangent[0]
    near, sends = neighbours[0], send_list[0, 0]
    core = lax.axis_index("core").astype(I32).reshape(1)
    table = jnp.asarray(TABLE)
    tile = (4, 64, 128)
    face = jax.ShapeDtypeStruct((144, 128), BF16)
    to_upper, to_lower = pl.pallas_call(
        pack_faces,
        name="pack_faces",
        grid=(1,),
        out_shape=[face, face],
        in_specs=[SMEM_SPEC, SMEM_SPEC, pl.BlockSpec(tile, lambda i: (0, 0, 0)), pl.BlockSpec(tile, lambda i: (0, 0, 3))],
        out_specs=[pl.BlockSpec((144, 128), lambda i: (0, 0))] * 2,
        compiler_params=pltpu.CompilerParams(vmem_limit_bytes=60 * 1024 * 1024),
    )(core, sends, feat, feat)
    from_lower, from_upper = passed_along(to_upper, 1), passed_along(to_lower, -1)

    fine = (8, 64, 512)
    pre, edges, up_back, ext0, cot_plane, cot_patch, w_adj, w_ups, w_dns = call(
        fine_inner, "fine_inner", 8,
        [(0, fine, F32), (0, (2, 64, 256), BF16), (0, (64, 1024), F32), (0, fine, BF16), (0, fine, BF16),
         (0, (512, 1024), BF16), (0, (192, 576), BF16), (0, (128, 256), BF16), (0, (128, 256), BF16)],
        [((576, 4096), BF16)],
        [near, table, w_fine, w_down, w_coarse, w_up, feat, cot],
    )
    hidden0, patch0, coarse_pre, hidden1, pre_edge, ext0_edge, to_upper, to_lower = call(
        fine_outer, "fine_outer", 4,
        [(0, fine, BF16), (0, (512, 1024), BF16), (0, (64, 1024), F32), (0, (64, 1024), BF16), (0, (2, 64, 512), F32),
         (0, (2, 64, 512), BF16), (0, (64, 256), BF16), (0, (64, 256), BF16)],
        [((576, 1024), BF16)],
        [near, table, from_lower, from_upper, edges, pre, w_fine, w_down],
    )
    low1, high1 = passed_along(to_upper, 1), passed_along(to_lower, -1)
    codes, ext1, conv, fine_slope, coarse_slope = call(
        coarse_inner, "coarse_inner", 4,
        [(0, (8, 256), I32), (0, (64, 1024), BF16), (0, (64, 1024), F32), (0, fine, F32), (0, (64, 1024), F32)],
        [((576, 1024), BF16)],
        [near, table, from_lower, from_upper, hidden1, pre, pre_edge, w_coarse, coarse_pre],
    )
    gated, delta_up, ext1_edge, to_upper, to_lower = call(
        coarse_outer, "coarse_outer", 3,
        [(0, (64, 1024), BF16), (0, (64, 1024), BF16), (0, (2, 64, 256), BF16), (0, (64, 256), BF16), (0, (64, 256), BF16)],
        [((576, 512), BF16)],
        [codes, hidden1, low1, high1, conv, up_back, w_coarse],
    )
    low2, high2 = passed_along(to_upper, 1), passed_along(to_lower, -1)
    decoded, grads_b, back = call(
        decode, "decode", 6,
        [(0, (4, 64, 512), BF16), (0, (1152, 128), F32), (0, (64, 1024), F32)],
        [((576, 1536), BF16), ((192, 1536), BF16), ((256, 1024), BF16)],
        [table, codes, gated, delta_up, ext1, ext1_edge, hidden0, cot_patch, w_ups, w_adj],
    )
    keep, send = call(
        finish, "finish", 12,
        [(0, (1152, 128), F32), (0, (1152, 128), BF16)],
        [((576, 512), BF16), ((256, 2048), BF16), ((576, 5120), BF16), ((192, 5120), BF16), ((1152, 128), F32)],
        [core, table, codes, delta_up, low2, high2, back, w_adj, coarse_slope, patch0, w_dns, fine_slope, cot_plane, ext0,
         ext0_edge, grads_b],
    )
    total = total_over_devices(keep, send)
    factor = 1.0 / math.sqrt(lax.axis_size(AXES) * 4 * 512)
    outs = call(
        lambda *refs: unfold(factor, *refs), "unfold", 3,
        [(0, w_fine.shape, F32), (0, w_down.shape, F32), (0, w_coarse.shape, F32), (0, w_up.shape, F32)], [], [core, total, other_core(total)],
    )
    return (decoded[None], *outs)


def solution(mesh):
    chips = mesh.devices.shape[0]
    x = min(4, chips)
    y = min(4, chips // x)
    grid = Mesh(mesh.devices.reshape(chips // (x * y), y, x, -1), AXES)
    in_specs = (
        P("core", CHIPS, None, None),
        P("core", CHIPS, None),
        P("core", CHIPS, None, None),
        P(),
        P(),
        P(),
        P(),
        P("core", CHIPS, None, None),
    )
    out_specs = (P("core", CHIPS, None, None), P(), P(), P(), P())
    return jax.shard_map(shards, mesh=grid, in_specs=in_specs, out_specs=out_specs, check_vma=False)
```

```python
import math

import jax
import jax.numpy as jnp
import numpy as np
from jax import lax
from jax.experimental import pallas as pl
from jax.experimental.pallas import tpu as pltpu
from jax.sharding import Mesh
from jax.sharding import PartitionSpec as P

F32 = jnp.float32
BF16 = jnp.bfloat16
I32 = jnp.int32
CHIPS = ("z", "y", "x")
AXES = ("z", "y", "x", "core")
FINE_SHIFTS = [10 * (c - 1) + (e - 1) for c in range(3) for e in range(3)]
COARSE_SHIFTS = [6 * (c - 1) + (e - 1) for c in range(3) for e in range(3)]


def lane_tables():
    table = np.full((16, 2048), -1, np.int32)
    t = np.arange(128)
    y, z, inside = t // 10 - 1, t % 10 - 1, t < 100
    c, e = np.where(y < 0, 0, np.where(y >= 8, 2, 1)), np.where(z < 0, 0, np.where(z >= 8, 2, 1))
    table[0, :128] = np.where(inside, 3 * c + e, -1)
    table[1, :128] = np.where(inside, (y - 8 * (c - 1)) * 8 + (z - 8 * (e - 1)), 0)
    own = inside & (c == 1) & (e == 1)
    for b in range(4):
        table[4, 128 * b : 128 * b + 128] = np.where(own, 64 * b + y * 8 + z, -1)
    u = np.arange(64)
    cy, cz, cin = u // 6 - 1, u % 6 - 1, u < 36
    cc, ce = np.where(cy < 0, 0, np.where(cy >= 4, 2, 1)), np.where(cz < 0, 0, np.where(cz >= 4, 2, 1))
    for b in range(2):
        at = slice(64 * b, 64 * b + 64)
        table[2, at] = np.where(cin, 3 * cc + ce, -1)
        table[3, at] = np.where(cin, 6 * (cy - 4 * (cc - 1) + 1) + cz - 4 * (ce - 1) + 1, 0)
    cown = cin & (cc == 1) & (ce == 1)
    w = np.arange(64)
    for j in range(2):
        for l in range(2):
            for b in range(2):
                at = (2 * j + l) * 128 + 64 * b
                rows = 128 * b + 10 * (2 * cy + j + 1) + 2 * cz + l + 1
                table[5, at : at + 64] = np.where(cown, rows, -1)
            for b in range(4):
                ny, nz = w // 8, w % 8
                hit = (ny % 2 == j) & (nz % 2 == l)
                at = (2 * j + l) * 256 + 64 * b
                table[7, at : at + 64] = np.where(hit, 64 * b + 6 * (ny // 2 + 1) + nz // 2 + 1, -1)
                hit = own & (y % 2 == j) & (z % 2 == l)
                at = (2 * j + l) * 512 + 128 * b
                table[8, at : at + 128] = np.where(hit, 64 * b + 6 * (y // 2 + 1) + z // 2 + 1, -1)
    real = np.flatnonzero(cown)
    for half in range(2):
        for b in range(4):
            table[9, 64 * half + 16 * b : 64 * half + 16 * b + 16] = 256 * half + 64 * b + real
            table[10, 256 * half + 64 * b + real] = 64 * half + 16 * b + np.arange(16)
    for b in range(2):
        table[6, 64 * b : 64 * b + 64] = 128 * b + 10 * (w // 8 + 1) + w % 8 + 1
    return table


TABLE = lane_tables()


def mm(a, b):
    return jnp.dot(a, b, preferred_element_type=F32)


def nt(a, b):
    return lax.dot_general(a, b, (((1,), (1,)), ((), ())), preferred_element_type=F32)


def roll(v, shift):
    return pltpu.roll(v, shift % 128, 1)


def onehot(code, rows):
    hit = lax.broadcasted_iota(I32, (rows, code.shape[1]), 0) == code
    return jnp.where(hit, 1.0, 0.0).astype(BF16)


def low_half(shape):
    return lax.broadcasted_iota(I32, shape, 1) < 64


def merge(low, first, second):
    return jnp.where(low, first, roll(second, 64))


def merge_high(low, first, second):
    return jnp.where(low, roll(first, 64), second)


def sigmoid(v):
    return 1.0 / (1.0 + jnp.exp(-v))


def silu(v):
    return v / (1.0 + jnp.exp(-v))


def slope(v):
    s = sigmoid(v)
    return s * (1.0 + v * (1.0 - s))


def raw_slots(neighbours, a, block, direction):
    found = jnp.full(direction.shape, -1, I32)
    for j in range(9):
        k = 9 * a + j
        entry = block if k == 13 else neighbours[block, k - (k > 13)]
        found = jnp.where(direction == j, entry, found)
    return found


def local_code(slots, cells):
    return jnp.where(slots >= 0, slots * 64 + cells, -1)


def edge_code(slots, cells, base, remote_slots):
    code = jnp.where((slots >= 0) & (slots < 4), slots * 64 + cells, -1)
    reach = (slots >= base) & (slots < base + 16)
    for j in range(4):
        hit = reach & (slots - base == remote_slots[j : j + 1])
        code = jnp.where(hit, 256 + j * 64 + cells, code)
    return code


def fine_slots(neighbours, table, a):
    direction = table[0:1, :128]
    return [raw_slots(neighbours, a, b, direction) for b in range(4)]


def coarse_slots(neighbours, table, a):
    direction = table[2:3, :128]
    low = low_half((1, 128))
    per_block = [raw_slots(neighbours, a, b, direction) for b in range(4)]
    return [jnp.where(low, per_block[0], per_block[1]), jnp.where(low, per_block[2], per_block[3])]


def arrived_slots(payload):
    return payload[128:144, :].astype(F32).astype(I32)


def tap_rows(w_ref):
    return jnp.concatenate([w_ref[:, 576 * a : 576 * a + 576] for a in range(3)], axis=0)


def put_taps(dst, at, plane, shifts):
    for s in range(plane.shape[1] // 128):
        piece = plane[:, 128 * s : 128 * s + 128]
        for j, shift in enumerate(shifts):
            moved = piece if shift == 0 else roll(piece, -shift)
            dst[64 * j : 64 * j + 64, at + 128 * s : at + 128 * s + 128] = moved


def natural_planes(ref):
    low = low_half((64, 128))
    planes = []
    for t in range(4):
        tiles = [ref[b, :, 128 * t : 128 * t + 128] for b in range(4)]
        planes.append(jnp.concatenate([merge(low, tiles[2 * p], tiles[2 * p + 1]) for p in range(2)], axis=1))
        planes.append(jnp.concatenate([merge_high(low, tiles[2 * p], tiles[2 * p + 1]) for p in range(2)], axis=1))
    return planes


def transposed_blocks(w, order):
    wt = w.astype(F32).T
    return jnp.concatenate([wt[64 * k : 64 * k + 64, :] for k in order], axis=1).astype(BF16)


def slot_of(sends, side, block):
    slot = jnp.int32(-1)
    for s in range(16):
        slot = jnp.where(sends[side, s] == block, s, slot)
    return slot


def pack_faces(core, sends, low_tile, high_tile, to_upper, to_lower):
    low = low_half((64, 128))
    for p in range(2):
        to_upper[64 * p : 64 * p + 64, :] = merge_high(low, high_tile[2 * p], high_tile[2 * p + 1])
        to_lower[64 * p : 64 * p + 64, :] = merge(low, low_tile[2 * p], low_tile[2 * p + 1])
    rows = lax.broadcasted_iota(I32, (16, 128), 0)
    for side, out in ((0, to_upper), (1, to_lower)):
        slots = jnp.full((16, 128), -1, I32)
        for j in range(4):
            slots = jnp.where(rows == j, slot_of(sends, side, j), slots)
        out[128:144, :] = slots.astype(F32).astype(BF16)


def fine_inner(neighbours, table, w_fine, w_down, w_coarse, w_up, feat, cot,
               pre, edges, up_back, ext, cot_plane, cot_patch, w_adj, w_ups, w_dns, taps):
    planes = natural_planes(feat)
    edges[0], edges[1] = planes[0], planes[7]
    cells = table[1:2, :128]
    code = jnp.concatenate([local_code(v, cells) for v in fine_slots(neighbours, table, 1)], axis=1)
    whole = mm(jnp.concatenate(planes, axis=0), onehot(code, 256)).astype(BF16)
    weight = tap_rows(w_fine)
    for x in range(8):
        plane = whole[64 * x : 64 * x + 64]
        ext[x] = plane
        put_taps(taps, 512 * x, plane, FINE_SHIFTS)
    for x in range(8):
        part = mm(weight, taps[:, 512 * x : 512 * x + 512])
        for a in range(3):
            out = x + 1 - a
            if 0 <= out < 8:
                piece = part[64 * a : 64 * a + 64]
                if x == max(out - 1, 0):
                    pre[out] = piece
                else:
                    pre[out] += piece
    placed = mm(jnp.concatenate(natural_planes(cot), axis=0), onehot(table[4:5, :512], 256)).astype(BF16)
    for x in range(8):
        cot_plane[x] = placed[64 * x : 64 * x + 64]
    down = onehot(table[5:6, :512], 256)
    for p in range(2):
        put_patches(cot_patch, mm(placed[:, 256 * p : 256 * p + 256], down).astype(BF16), p)
    up_back[...] = mm(w_up[...], cot_patch[...])
    for a in range(3):
        order = [(2 - a) * 9 + 8 - j for j in range(9)]
        w_adj[64 * a : 64 * a + 64, :] = transposed_blocks(w_coarse[...], order)
    for i in range(2):
        w_ups[64 * i : 64 * i + 64, :] = transposed_blocks(w_up[...], range(4 * i, 4 * i + 4))
        w_dns[64 * i : 64 * i + 64, :] = transposed_blocks(w_down[...], range(4 * i, 4 * i + 4))


def put_patches(dst, selected, pair):
    for x in range(8):
        for jl in range(4):
            at = ((x % 2) * 4 + jl) * 64
            lane = (x // 2) * 256 + pair * 128
            dst[at : at + 64, lane : lane + 128] = selected[64 * x : 64 * x + 64, 128 * jl : 128 * jl + 128]


def boundary(table, hidden1, up_back, edge, inner):
    exact = up_back[:, 256 * edge : 256 * edge + 256]
    high = exact.astype(BF16)
    low = (exact - high.astype(F32)).astype(BF16)
    top = jnp.concatenate([hidden1[:, 256 * p : 256 * p + 256] for p in (edge, inner)], axis=1)
    both = jnp.concatenate([top, jnp.concatenate([high, low], axis=1)], axis=0)
    return mm(both, onehot(table[9:10, :128], 512)).astype(BF16)


def fine_outer(neighbours, table, from_lower, from_upper, edges, pre, w_fine, w_down, up_back,
               hidden, patch, coarse_pre, hidden1, pre_edge, ext_edge, to_upper, to_lower, taps):
    cells = table[1:2, :128]
    weight = tap_rows(w_fine)
    for side, a, base, payload in ((0, 0, 4, from_lower), (1, 2, 20, from_upper)):
        slots = arrived_slots(payload)
        code = jnp.concatenate([edge_code(v, cells, base, slots) for v in fine_slots(neighbours, table, a)], axis=1)
        pool = jnp.concatenate([edges[1 - side], payload[0:64, :], payload[64:128, :]], axis=1)
        plane = mm(pool, onehot(code, 512)).astype(BF16)
        ext_edge[side] = plane
        put_taps(taps, 512 * side, plane, FINE_SHIFTS)
        part = mm(weight[64 * a : 64 * a + 64], taps[:, 512 * side : 512 * side + 512])
        pre_edge[side] = pre[7 * side] + part
    for x in range(8):
        value = pre_edge[0] if x == 0 else pre_edge[1] if x == 7 else pre[x]
        hidden[x] = silu(value).astype(BF16)
    down = onehot(table[5:6, :512], 256)
    for p in range(2):
        rows = jnp.concatenate([hidden[x, :, 256 * p : 256 * p + 256] for x in range(8)], axis=0)
        put_patches(patch, mm(rows, down).astype(BF16), p)
    value = mm(w_down[...], patch[...])
    coarse_pre[...] = value
    value = silu(value).astype(BF16)
    hidden1[...] = value
    exact = up_back[...]
    to_upper[...] = boundary(table, value, exact, 3, 2)
    to_lower[...] = boundary(table, value, exact, 0, 1)


def by_rows(v):
    return jnp.concatenate([v[:, 256 * x : 256 * x + 256] for x in range(4)], axis=0)


def coarse_inner_conv(field, select, weight, taps, ext):
    whole = mm(by_rows(field), select).astype(BF16)
    for x in range(4):
        plane = whole[64 * x : 64 * x + 64]
        if ext is not None:
            ext[:, 256 * x : 256 * x + 256] = plane
        put_taps(taps, 256 * x, plane, COARSE_SHIFTS)
    part = mm(weight, taps[:, :1024])
    sums = []
    for x in range(4):
        total = part[64:128, 256 * x : 256 * x + 256]
        if x > 0:
            total = total + part[0:64, 256 * x - 256 : 256 * x]
        if x < 3:
            total = total + part[128:192, 256 * x + 256 : 256 * x + 512]
        sums.append(total)
    return jnp.concatenate(sums, axis=1)


def coarse_outer_conv(codes, side, own_plane, arrived, weight, taps, at):
    pool = jnp.concatenate([own_plane, arrived], axis=1)
    plane = mm(pool, onehot(codes[side : side + 1, :], 512)).astype(BF16)
    put_taps(taps, at, plane, COARSE_SHIFTS)
    return mm(weight[128 * side : 128 * side + 64], taps[:, at : at + 256]), plane


def peer_codes(table, slots, own_slots):
    direction, cells = table[2:3, :128], table[3:4, :128]
    low = low_half((1, 128))
    down = jnp.where(direction >= 6, 1, jnp.where(direction >= 3, 0, -1))
    across = direction - 3 * (down + 1) - 1
    codes = ([], [])
    for pair in range(2):
        place = jnp.where(low, slots[2 * pair : 2 * pair + 1], slots[2 * pair + 1 : 2 * pair + 2])
        y, z = (place >> 2) + down, (place & 3) + across
        inside = (direction >= 0) & (y >= 0) & (y < 4) & (z >= 0) & (z < 4)
        wanted = jnp.where(inside, y * 4 + z, -2)
        for found, candidates in zip(codes, ([slots[j : j + 1] for j in range(4)], own_slots)):
            code = jnp.full((1, 128), -1, I32)
            for j in range(4):
                code = jnp.where(wanted == candidates[j], 64 * j + cells, code)
            found.append(code)
    return [jnp.concatenate(code, axis=1) for code in codes]


def coarse_inner(neighbours, sends, table, from_lower, from_upper, hidden1, pre, pre_edge, w_coarse, coarse_pre,
                 codes, ext, conv, fine_slope, coarse_slope, taps):
    coarse_slope[...] = slope(coarse_pre[...])
    cells = table[3:4, :128]
    for row, a, base, payload in ((0, 0, 4, from_lower), (1, 2, 20, from_upper)):
        slots = arrived_slots(payload)
        code = [edge_code(v, cells, base, slots) for v in coarse_slots(neighbours, table, a)]
        codes[row : row + 1, :] = jnp.concatenate(code, axis=1)
        theirs, ours = peer_codes(table, slots, [slot_of(sends, 1 - row, m) for m in range(4)])
        codes[3 + row : 4 + row, :] = theirs
        codes[5 + row : 6 + row, :] = ours
    code = [local_code(v, cells) for v in coarse_slots(neighbours, table, 1)]
    codes[2:3, :] = jnp.concatenate(code, axis=1)
    codes[7:8, :] = jnp.full((1, 256), -1, I32)
    select = onehot(codes[2:3, :], 256)
    conv[...] = coarse_inner_conv(hidden1[...], select, tap_rows(w_coarse), taps, ext)
    for x in range(8):
        value = pre_edge[0] if x == 0 else pre_edge[1] if x == 7 else pre[x]
        fine_slope[x] = slope(value)


def coarse_outer(codes, table, hidden1, from_lower, from_upper, conv, up_back, w_coarse,
                 gated, delta, ext_edge, delta_lower, delta_upper, taps, peer_taps):
    weight = tap_rows(w_coarse)
    spread = onehot(table[10:11, :512], 128)
    edge = []
    for side, payload, own, result in (
        (0, from_lower, hidden1[:, 768:], delta_lower),
        (1, from_upper, hidden1[:, :256], delta_upper),
    ):
        full = mm(payload[...], spread)
        top = full[:64].astype(BF16)
        part, ext_edge[side] = coarse_outer_conv(codes, side, own, top[:, :256], weight, taps, 256 * side)
        edge.append(part)
        select = onehot(codes[3 + side : 4 + side, :], 256)
        rows = mm(jnp.concatenate([top[:, :256], top[:, 256:]], axis=0), select).astype(BF16)
        facing = hidden1[:, :256] if side == 0 else hidden1[:, 768:]
        beyond = mm(facing, onehot(codes[5 + side : 6 + side, :], 256)).astype(BF16)
        order = (rows[64:], rows[:64], beyond) if side == 0 else (beyond, rows[:64], rows[64:])
        for a, plane in enumerate(order):
            put_taps(peer_taps.at[576 * a : 576 * a + 576], 256 * side, plane, COARSE_SHIFTS)
        value = mm(w_coarse[...], peer_taps[:, 256 * side : 256 * side + 256])
        result[...] = ((full[64:, :256] + full[64:, 256:]) * slope(value)).astype(BF16)
    value = conv[...]
    value = jnp.concatenate([value[:, :256] + edge[0], value[:, 256:768], value[:, 768:] + edge[1]], axis=1)
    gated[...] = silu(value).astype(BF16)
    delta[...] = (up_back[...] * slope(value)).astype(BF16)


def decode(table, codes, gated, delta, ext, ext_edge, hidden, cot_patch, w_ups, w_adj,
           decoded, grads, back, taps, stack, spread):
    select = onehot(codes[2:3, :], 256)
    back[...] = coarse_inner_conv(delta[...], select, w_adj[...], taps, None)
    chosen = mm(by_rows(gated[...]), onehot(table[7:8, :1024], 256)).astype(BF16)
    for x in range(4):
        for jl in range(4):
            spread[64 * jl : 64 * jl + 64, 256 * x : 256 * x + 256] = (
                chosen[64 * x : 64 * x + 64, 256 * jl : 256 * jl + 256]
            )
    up = mm(w_ups[...], spread[...])
    compress = onehot(table[6:7, :128], 256)
    low = low_half((64, 128))
    for p in range(2):
        rows = jnp.concatenate([hidden[x, :, 256 * p : 256 * p + 256] for x in range(8)], axis=0)
        own = mm(rows, compress)
        for t in range(4):
            even, odd = [
                own[64 * x : 64 * x + 64] + up[64 * i : 64 * i + 64, 256 * t + 128 * p : 256 * t + 128 * p + 128]
                for i, x in ((0, 2 * t), (1, 2 * t + 1))
            ]
            decoded[2 * p, :, 128 * t : 128 * t + 128] = merge(low, even, odd).astype(BF16)
            decoded[2 * p + 1, :, 128 * t : 128 * t + 128] = merge_high(low, even, odd).astype(BF16)
    put_taps(taps, 0, ext_edge[0], COARSE_SHIFTS)
    for x in range(4):
        put_taps(taps, 256 + 256 * x, ext[:, 256 * x : 256 * x + 256], COARSE_SHIFTS)
    put_taps(taps, 1280, ext_edge[1], COARSE_SHIFTS)
    stack[...] = jnp.zeros(stack.shape, BF16)
    for a in range(3):
        stack[64 * a : 64 * a + 64, 256 * a : 256 * a + 1024] = delta[...]
    of_coarse = nt(taps[...], stack[...])
    of_up = jnp.concatenate([nt(cot_patch[...], gated[...]), jnp.zeros((64, 64), F32)], axis=0)
    put_grads(grads, of_coarse, of_up)


def finish(core, table, codes, delta, from_lower, from_upper, back, w_adj, coarse_slope, patch, w_dns, fine_slope,
           cot_plane, ext, ext_edge, grads_b, keep, send, coarse_taps, spread, taps, stack, grads):
    weight = w_adj[...]
    low, _ = coarse_outer_conv(codes, 0, delta[:, 768:], from_lower[...], weight, coarse_taps, 0)
    high, _ = coarse_outer_conv(codes, 1, delta[:, :256], from_upper[...], weight, coarse_taps, 256)
    value = back[...]
    value = jnp.concatenate([value[:, :256] + low, value[:, 256:768], value[:, 768:] + high], axis=1)
    down = (value * coarse_slope[...]).astype(BF16)
    of_down = jnp.concatenate([nt(patch[...], down), jnp.zeros((64, 64), F32)], axis=0)
    chosen = mm(by_rows(down), onehot(table[8:9, :2048], 256)).astype(BF16)
    for x in range(4):
        for jl in range(4):
            spread[64 * jl : 64 * jl + 64, 512 * x : 512 * x + 512] = (
                chosen[64 * x : 64 * x + 64, 512 * jl : 512 * jl + 512]
            )
    for a in range(3):
        for plane in range(10):
            if not 0 <= plane - a < 8:
                stack[64 * a : 64 * a + 64, 512 * plane : 512 * plane + 512] = jnp.zeros((64, 512), BF16)
    for half in range(4):
        raised = mm(w_dns[...], spread[:, 512 * half : 512 * half + 512])
        for i in range(2):
            x = 2 * half + i
            total = cot_plane[x].astype(F32) + raised[64 * i : 64 * i + 64]
            fine = (total * fine_slope[x]).astype(BF16)
            for a in range(3):
                at = 512 * (x + a)
                stack[64 * a : 64 * a + 64, at : at + 512] = fine
    put_taps(taps, 0, ext_edge[0], FINE_SHIFTS)
    for x in range(8):
        put_taps(taps, 512 * x + 512, ext[x], FINE_SHIFTS)
    put_taps(taps, 4608, ext_edge[1], FINE_SHIFTS)
    put_grads(grads, nt(taps[...], stack[...]), of_down)
    first = core[0] == 0

    @pl.when(first)
    def _():
        keep[...] = grads[...]
        send[...] = grads_b[...].astype(BF16)

    @pl.when(jnp.logical_not(first))
    def _():
        keep[...] = grads_b[...]
        send[...] = grads[...].astype(BF16)


def put_grads(grads, wide, narrow):
    grads[0:576, :] = wide[:, :128]
    grads[576:1152, :] = jnp.concatenate([wide[:, 128:], narrow], axis=1)


def unfold(factor, core, own, other, grad_fine, grad_down, grad_coarse, grad_up):
    def spell(half, wide, narrow):
        both = jnp.concatenate([half[0:576, :], half[576:1152, :]], axis=1)
        turned = (both.astype(F32) * factor).T
        wide[...] = jnp.concatenate([turned[64 * a : 64 * a + 64, :] for a in range(3)], axis=1)
        narrow[...] = turned[192:256, :512]

    first = core[0] == 0

    @pl.when(first)
    def _():
        spell(own, grad_fine, grad_down)
        spell(other, grad_coarse, grad_up)

    @pl.when(jnp.logical_not(first))
    def _():
        spell(other, grad_fine, grad_down)
        spell(own, grad_coarse, grad_up)


VMEM_SPEC = pl.BlockSpec(memory_space=pltpu.VMEM)
SMEM_SPEC = pl.BlockSpec(memory_space=pltpu.SMEM)
HBM_SPEC = pl.BlockSpec(memory_space=pltpu.HBM)


def call(kernel, name, megabytes, outs, scratch, near, far=(), late=False):
    counts = (len(near), len(far), len(outs), len(scratch), len(far))
    far_outs = [k for k, (away, _, _) in enumerate(outs) if away]

    def body(*refs):
        groups, at = [], 0
        for count in counts:
            groups.append(refs[at : at + count])
            at += count
        near_refs, far_refs, out_refs, own, landed = groups
        staged, (in_sem, out_sem) = refs[at : at + len(far_outs)], refs[at + len(far_outs) :]
        arriving = [pltpu.make_async_copy(s, d, in_sem.at[k]) for k, (s, d) in enumerate(zip(far_refs, landed))]
        for copy in arriving:
            copy.start()
        results = list(out_refs)
        for k, buffer in zip(far_outs, staged):
            results[k] = buffer
        if late:
            kernel([copy.wait for copy in arriving], *near_refs, *landed, *results, *own)
        else:
            for copy in arriving:
                copy.wait()
            kernel(*near_refs, *landed, *results, *own)
        leaving = [
            pltpu.make_async_copy(buffer, out_refs[k], out_sem.at[n])
            for n, (k, buffer) in enumerate(zip(far_outs, staged))
        ]
        for copy in leaving:
            copy.start()
        for copy in leaving:
            copy.wait()

    small = ((4, 26), (2, 16), (1,))
    return pl.pallas_call(
        body,
        name=name,
        out_shape=[jax.ShapeDtypeStruct(shape, kind) for _, shape, kind in outs],
        in_specs=[SMEM_SPEC if x.shape in small else VMEM_SPEC for x in near] + [HBM_SPEC] * len(far),
        out_specs=[HBM_SPEC if away else VMEM_SPEC for away, _, _ in outs],
        scratch_shapes=[pltpu.VMEM(shape, kind) for shape, kind in scratch]
        + [pltpu.VMEM(x.shape, x.dtype) for x in far]
        + [pltpu.VMEM(outs[k][1], outs[k][2]) for k in far_outs]
        + [pltpu.SemaphoreType.DMA((max(len(far), 1),)), pltpu.SemaphoreType.DMA((max(len(far_outs), 1),))],
        compiler_params=pltpu.CompilerParams(vmem_limit_bytes=megabytes * 1024 * 1024),
    )(*near, *far)


def passed_along(block, distance):
    devices = range(lax.axis_size(CHIPS))
    route = [(i - distance, i) for i in devices if i - distance in devices]
    return lax.ppermute(block, CHIPS, route)


def other_core(x):
    return lax.ppermute(x, "core", [(0, 1), (1, 0)])


def dealt(x, axes):
    count = lax.axis_size(axes)
    return lax.all_to_all(x.reshape(count, -1, 128), axes, 0, 0, tiled=True)


def told(x, axes):
    return dealt(jnp.broadcast_to(x, (lax.axis_size(axes), *x.shape)), axes)


def summed(blocks):
    total = blocks[0].astype(F32)
    for k in range(1, blocks.shape[0]):
        total = total + blocks[k].astype(F32)
    return total


def total_over_devices(keep, send):
    x = keep + other_core(send).astype(F32)
    x = summed(dealt(x.astype(BF16), ("y", "x")))
    x = summed(told(x.astype(BF16), "z"))
    return told(x.astype(BF16), ("y", "x")).reshape(keep.shape)


def shards(features, neighbours, send_list, w_fine, w_down, w_coarse, w_up, cotangent):
    feat, cot = features[0], cotangent[0]
    near, sends = neighbours[0], send_list[0, 0]
    core = lax.axis_index("core").astype(I32).reshape(1)
    table = jnp.asarray(TABLE)
    tile = (4, 64, 128)
    face = jax.ShapeDtypeStruct((144, 128), BF16)
    to_upper, to_lower = pl.pallas_call(
        pack_faces,
        name="pack_faces",
        grid=(1,),
        out_shape=[face, face],
        in_specs=[SMEM_SPEC, SMEM_SPEC, pl.BlockSpec(tile, lambda i: (0, 0, 0)), pl.BlockSpec(tile, lambda i: (0, 0, 3))],
        out_specs=[pl.BlockSpec((144, 128), lambda i: (0, 0))] * 2,
        compiler_params=pltpu.CompilerParams(vmem_limit_bytes=60 * 1024 * 1024),
    )(core, sends, feat, feat)
    from_lower, from_upper = passed_along(to_upper, 1), passed_along(to_lower, -1)

    fine = (8, 64, 512)
    pre, edges, up_back, ext0, cot_plane, cot_patch, w_adj, w_ups, w_dns = call(
        fine_inner, "fine_inner", 8,
        [(0, fine, F32), (0, (2, 64, 256), BF16), (0, (64, 1024), F32), (0, fine, BF16), (0, fine, BF16),
         (0, (512, 1024), BF16), (0, (192, 576), BF16), (0, (128, 256), BF16), (0, (128, 256), BF16)],
        [((576, 4096), BF16)],
        [near, table, w_fine, w_down, w_coarse, w_up, feat, cot],
    )
    hidden0, patch0, coarse_pre, hidden1, pre_edge, ext0_edge, to_upper, to_lower = call(
        fine_outer, "fine_outer", 4,
        [(0, fine, BF16), (0, (512, 1024), BF16), (0, (64, 1024), F32), (0, (64, 1024), BF16), (0, (2, 64, 512), F32),
         (0, (2, 64, 512), BF16), (0, (128, 128), BF16), (0, (128, 128), BF16)],
        [((576, 1024), BF16)],
        [near, table, from_lower, from_upper, edges, pre, w_fine, w_down, up_back],
    )
    low1, high1 = passed_along(to_upper, 1), passed_along(to_lower, -1)
    codes, ext1, conv, fine_slope, coarse_slope = call(
        coarse_inner, "coarse_inner", 4,
        [(0, (8, 256), I32), (0, (64, 1024), BF16), (0, (64, 1024), F32), (0, fine, F32), (0, (64, 1024), F32)],
        [((576, 1024), BF16)],
        [near, sends, table, from_lower, from_upper, hidden1, pre, pre_edge, w_coarse, coarse_pre],
    )
    gated, delta_up, ext1_edge, low2, high2 = call(
        coarse_outer, "coarse_outer", 5,
        [(0, (64, 1024), BF16), (0, (64, 1024), BF16), (0, (2, 64, 256), BF16), (0, (64, 256), BF16), (0, (64, 256), BF16)],
        [((576, 512), BF16), ((1728, 512), BF16)],
        [codes, table, hidden1, low1, high1, conv, up_back, w_coarse],
    )
    decoded, grads_b, back = call(
        decode, "decode", 6,
        [(0, (4, 64, 512), BF16), (0, (1152, 128), F32), (0, (64, 1024), F32)],
        [((576, 1536), BF16), ((192, 1536), BF16), ((256, 1024), BF16)],
        [table, codes, gated, delta_up, ext1, ext1_edge, hidden0, cot_patch, w_ups, w_adj],
    )
    keep, send = call(
        finish, "finish", 12,
        [(0, (1152, 128), F32), (0, (1152, 128), BF16)],
        [((576, 512), BF16), ((256, 2048), BF16), ((576, 5120), BF16), ((192, 5120), BF16), ((1152, 128), F32)],
        [core, table, codes, delta_up, low2, high2, back, w_adj, coarse_slope, patch0, w_dns, fine_slope, cot_plane, ext0,
         ext0_edge, grads_b],
    )
    total = total_over_devices(keep, send)
    factor = 1.0 / math.sqrt(lax.axis_size(AXES) * 4 * 512)
    outs = call(
        lambda *refs: unfold(factor, *refs), "unfold", 3,
        [(0, w_fine.shape, F32), (0, w_down.shape, F32), (0, w_coarse.shape, F32), (0, w_up.shape, F32)], [], [core, total, other_core(total)],
    )
    return (decoded[None], *outs)


def solution(mesh):
    chips = mesh.devices.shape[0]
    x = min(4, chips)
    y = min(4, chips // x)
    grid = Mesh(mesh.devices.reshape(chips // (x * y), y, x, -1), AXES)
    in_specs = (
        P("core", CHIPS, None, None),
        P("core", CHIPS, None),
        P("core", CHIPS, None, None),
        P(),
        P(),
        P(),
        P(),
        P("core", CHIPS, None, None),
    )
    out_specs = (P("core", CHIPS, None, None), P(), P(), P(), P())
    return jax.shard_map(shards, mesh=grid, in_specs=in_specs, out_specs=out_specs, check_vma=False)
```

```python
import math

import jax
import jax.numpy as jnp
import numpy as np
from jax import lax
from jax.experimental import pallas as pl
from jax.experimental.pallas import tpu as pltpu
from jax.sharding import Mesh
from jax.sharding import PartitionSpec as P

F32 = jnp.float32
BF16 = jnp.bfloat16
I32 = jnp.int32
CHIPS = ("z", "y", "x")
AXES = ("z", "y", "x", "core")
FINE_SHIFTS = [10 * (c - 1) + (e - 1) for c in range(3) for e in range(3)]
COARSE_SHIFTS = [6 * (c - 1) + (e - 1) for c in range(3) for e in range(3)]


def lane_tables():
    table = np.full((16, 2048), -1, np.int32)
    t = np.arange(128)
    y, z, inside = t // 10 - 1, t % 10 - 1, t < 100
    c, e = np.where(y < 0, 0, np.where(y >= 8, 2, 1)), np.where(z < 0, 0, np.where(z >= 8, 2, 1))
    table[0, :128] = np.where(inside, 3 * c + e, -1)
    table[1, :128] = np.where(inside, (y - 8 * (c - 1)) * 8 + (z - 8 * (e - 1)), 0)
    own = inside & (c == 1) & (e == 1)
    for b in range(4):
        table[4, 128 * b : 128 * b + 128] = np.where(own, 64 * b + y * 8 + z, -1)
    u = np.arange(64)
    cy, cz, cin = u // 6 - 1, u % 6 - 1, u < 36
    cc, ce = np.where(cy < 0, 0, np.where(cy >= 4, 2, 1)), np.where(cz < 0, 0, np.where(cz >= 4, 2, 1))
    for b in range(2):
        at = slice(64 * b, 64 * b + 64)
        table[2, at] = np.where(cin, 3 * cc + ce, -1)
        table[3, at] = np.where(cin, 6 * (cy - 4 * (cc - 1) + 1) + cz - 4 * (ce - 1) + 1, 0)
    cown = cin & (cc == 1) & (ce == 1)
    w = np.arange(64)
    for j in range(2):
        for l in range(2):
            for b in range(2):
                at = (2 * j + l) * 128 + 64 * b
                rows = 128 * b + 10 * (2 * cy + j + 1) + 2 * cz + l + 1
                table[5, at : at + 64] = np.where(cown, rows, -1)
            for b in range(4):
                ny, nz = w // 8, w % 8
                hit = (ny % 2 == j) & (nz % 2 == l)
                at = (2 * j + l) * 256 + 64 * b
                table[7, at : at + 64] = np.where(hit, 64 * b + 6 * (ny // 2 + 1) + nz // 2 + 1, -1)
                hit = own & (y % 2 == j) & (z % 2 == l)
                at = (2 * j + l) * 512 + 128 * b
                table[8, at : at + 128] = np.where(hit, 64 * b + 6 * (y // 2 + 1) + z // 2 + 1, -1)
    real = np.flatnonzero(cown)
    for half in range(2):
        for b in range(4):
            table[9, 64 * half + 16 * b : 64 * half + 16 * b + 16] = 256 * half + 64 * b + real
            table[10, 256 * half + 64 * b + real] = 64 * half + 16 * b + np.arange(16)
    for b in range(2):
        table[6, 64 * b : 64 * b + 64] = 128 * b + 10 * (w // 8 + 1) + w % 8 + 1
    return table


TABLE = lane_tables()


def mm(a, b):
    return jnp.dot(a, b, preferred_element_type=F32)


def nt(a, b):
    return lax.dot_general(a, b, (((1,), (1,)), ((), ())), preferred_element_type=F32)


def roll(v, shift):
    return pltpu.roll(v, shift % 128, 1)


def onehot(code, rows):
    hit = lax.broadcasted_iota(I32, (rows, code.shape[1]), 0) == code
    return jnp.where(hit, 1.0, 0.0).astype(BF16)


def low_half(shape):
    return lax.broadcasted_iota(I32, shape, 1) < 64


def merge(low, first, second):
    return jnp.where(low, first, roll(second, 64))


def merge_high(low, first, second):
    return jnp.where(low, roll(first, 64), second)


def sigmoid(v):
    return 1.0 / (1.0 + jnp.exp(-v))


def silu(v):
    return v / (1.0 + jnp.exp(-v))


def slope(v):
    s = sigmoid(v)
    return s * (1.0 + v * (1.0 - s))


def raw_slots(neighbours, a, block, direction):
    found = jnp.full(direction.shape, -1, I32)
    for j in range(9):
        k = 9 * a + j
        entry = block if k == 13 else neighbours[block, k - (k > 13)]
        found = jnp.where(direction == j, entry, found)
    return found


def local_code(slots, cells):
    return jnp.where(slots >= 0, slots * 64 + cells, -1)


def edge_code(slots, cells, base, remote_slots):
    code = jnp.where((slots >= 0) & (slots < 4), slots * 64 + cells, -1)
    reach = (slots >= base) & (slots < base + 16)
    for j in range(4):
        hit = reach & (slots - base == remote_slots[j : j + 1])
        code = jnp.where(hit, 256 + j * 64 + cells, code)
    return code


def fine_slots(neighbours, table, a):
    direction = table[0:1, :128]
    return [raw_slots(neighbours, a, b, direction) for b in range(4)]


def coarse_slots(neighbours, table, a):
    direction = table[2:3, :128]
    low = low_half((1, 128))
    per_block = [raw_slots(neighbours, a, b, direction) for b in range(4)]
    return [jnp.where(low, per_block[0], per_block[1]), jnp.where(low, per_block[2], per_block[3])]


def arrived_slots(payload):
    return payload[128:144, :].astype(F32).astype(I32)


def tap_rows(w_ref):
    return jnp.concatenate([w_ref[:, 576 * a : 576 * a + 576] for a in range(3)], axis=0)


def put_taps(dst, at, plane, shifts):
    for s in range(plane.shape[1] // 128):
        piece = plane[:, 128 * s : 128 * s + 128]
        for j, shift in enumerate(shifts):
            moved = piece if shift == 0 else roll(piece, -shift)
            dst[64 * j : 64 * j + 64, at + 128 * s : at + 128 * s + 128] = moved


def natural_planes(ref):
    low = low_half((64, 128))
    planes = []
    for t in range(4):
        tiles = [ref[b, :, 128 * t : 128 * t + 128] for b in range(4)]
        planes.append(jnp.concatenate([merge(low, tiles[2 * p], tiles[2 * p + 1]) for p in range(2)], axis=1))
        planes.append(jnp.concatenate([merge_high(low, tiles[2 * p], tiles[2 * p + 1]) for p in range(2)], axis=1))
    return planes


def transposed_blocks(w, order):
    wt = w.astype(F32).T
    return jnp.concatenate([wt[64 * k : 64 * k + 64, :] for k in order], axis=1).astype(BF16)


def slot_of(sends, side, block):
    slot = jnp.int32(-1)
    for s in range(16):
        slot = jnp.where(sends[side, s] == block, s, slot)
    return slot


def pack_faces(core, sends, low_tile, high_tile, to_upper, to_lower):
    low = low_half((64, 128))
    for p in range(2):
        to_upper[64 * p : 64 * p + 64, :] = merge_high(low, high_tile[2 * p], high_tile[2 * p + 1])
        to_lower[64 * p : 64 * p + 64, :] = merge(low, low_tile[2 * p], low_tile[2 * p + 1])
    rows = lax.broadcasted_iota(I32, (16, 128), 0)
    for side, out in ((0, to_upper), (1, to_lower)):
        slots = jnp.full((16, 128), -1, I32)
        for j in range(4):
            slots = jnp.where(rows == j, slot_of(sends, side, j), slots)
        out[128:144, :] = slots.astype(F32).astype(BF16)


def fine_inner(neighbours, table, w_fine, w_down, w_coarse, w_up, feat, cot,
               pre, edges, up_back, taps, cot_plane, cot_patch, w_adj, w_ups, w_dns):
    planes = natural_planes(feat)
    edges[0], edges[1] = planes[0], planes[7]
    cells = table[1:2, :128]
    code = jnp.concatenate([local_code(v, cells) for v in fine_slots(neighbours, table, 1)], axis=1)
    whole = mm(jnp.concatenate(planes, axis=0), onehot(code, 256)).astype(BF16)
    weight = tap_rows(w_fine)
    for x in range(8):
        plane = whole[64 * x : 64 * x + 64]
        put_taps(taps, 512 * x, plane, FINE_SHIFTS)
    for x in range(8):
        part = mm(weight, taps[:, 512 * x : 512 * x + 512])
        for a in range(3):
            out = x + 1 - a
            if 0 <= out < 8:
                piece = part[64 * a : 64 * a + 64]
                if x == max(out - 1, 0):
                    pre[out] = piece
                else:
                    pre[out] += piece
    placed = mm(jnp.concatenate(natural_planes(cot), axis=0), onehot(table[4:5, :512], 256)).astype(BF16)
    for x in range(8):
        cot_plane[x] = placed[64 * x : 64 * x + 64]
    down = onehot(table[5:6, :512], 256)
    for p in range(2):
        put_patches(cot_patch, mm(placed[:, 256 * p : 256 * p + 256], down).astype(BF16), p)
    up_back[...] = mm(w_up[...], cot_patch[...])
    for a in range(3):
        order = [(2 - a) * 9 + 8 - j for j in range(9)]
        w_adj[64 * a : 64 * a + 64, :] = transposed_blocks(w_coarse[...], order)
    for i in range(2):
        w_ups[64 * i : 64 * i + 64, :] = transposed_blocks(w_up[...], range(4 * i, 4 * i + 4))
        w_dns[64 * i : 64 * i + 64, :] = transposed_blocks(w_down[...], range(4 * i, 4 * i + 4))


def put_patches(dst, selected, pair):
    for x in range(8):
        for jl in range(4):
            at = ((x % 2) * 4 + jl) * 64
            lane = (x // 2) * 256 + pair * 128
            dst[at : at + 64, lane : lane + 128] = selected[64 * x : 64 * x + 64, 128 * jl : 128 * jl + 128]


def boundary(table, hidden1, up_back, edge, inner):
    exact = up_back[:, 256 * edge : 256 * edge + 256]
    high = exact.astype(BF16)
    low = (exact - high.astype(F32)).astype(BF16)
    top = jnp.concatenate([hidden1[:, 256 * p : 256 * p + 256] for p in (edge, inner)], axis=1)
    both = jnp.concatenate([top, jnp.concatenate([high, low], axis=1)], axis=0)
    return mm(both, onehot(table[9:10, :128], 512)).astype(BF16)


def fine_outer(neighbours, table, from_lower, from_upper, edges, pre, w_fine, w_down, up_back,
               hidden, patch, coarse_pre, hidden1, pre_edge, taps, to_upper, to_lower):
    cells = table[1:2, :128]
    weight = tap_rows(w_fine)
    for side, a, base, payload in ((0, 0, 4, from_lower), (1, 2, 20, from_upper)):
        slots = arrived_slots(payload)
        code = jnp.concatenate([edge_code(v, cells, base, slots) for v in fine_slots(neighbours, table, a)], axis=1)
        pool = jnp.concatenate([edges[1 - side], payload[0:64, :], payload[64:128, :]], axis=1)
        plane = mm(pool, onehot(code, 512)).astype(BF16)
        put_taps(taps, 512 * side, plane, FINE_SHIFTS)
        part = mm(weight[64 * a : 64 * a + 64], taps[:, 512 * side : 512 * side + 512])
        pre_edge[side] = pre[7 * side] + part
    for x in range(8):
        value = pre_edge[0] if x == 0 else pre_edge[1] if x == 7 else pre[x]
        hidden[x] = silu(value).astype(BF16)
    down = onehot(table[5:6, :512], 256)
    for p in range(2):
        rows = jnp.concatenate([hidden[x, :, 256 * p : 256 * p + 256] for x in range(8)], axis=0)
        put_patches(patch, mm(rows, down).astype(BF16), p)
    value = mm(w_down[...], patch[...])
    coarse_pre[...] = value
    value = silu(value).astype(BF16)
    hidden1[...] = value
    exact = up_back[...]
    to_upper[...] = boundary(table, value, exact, 3, 2)
    to_lower[...] = boundary(table, value, exact, 0, 1)


def by_rows(v):
    return jnp.concatenate([v[:, 256 * x : 256 * x + 256] for x in range(4)], axis=0)


def coarse_inner_conv(field, select, weight, taps):
    whole = mm(by_rows(field), select).astype(BF16)
    for x in range(4):
        plane = whole[64 * x : 64 * x + 64]
        put_taps(taps, 256 * x, plane, COARSE_SHIFTS)
    part = mm(weight, taps[:, :1024])
    sums = []
    for x in range(4):
        total = part[64:128, 256 * x : 256 * x + 256]
        if x > 0:
            total = total + part[0:64, 256 * x - 256 : 256 * x]
        if x < 3:
            total = total + part[128:192, 256 * x + 256 : 256 * x + 512]
        sums.append(total)
    return jnp.concatenate(sums, axis=1)


def coarse_outer_conv(codes, side, own_plane, arrived, weight, taps, at):
    pool = jnp.concatenate([own_plane, arrived], axis=1)
    plane = mm(pool, onehot(codes[side : side + 1, :], 512)).astype(BF16)
    put_taps(taps, at, plane, COARSE_SHIFTS)
    return mm(weight[128 * side : 128 * side + 64], taps[:, at : at + 256])


def peer_codes(table, slots, own_slots):
    direction, cells = table[2:3, :128], table[3:4, :128]
    low = low_half((1, 128))
    down = jnp.where(direction >= 6, 1, jnp.where(direction >= 3, 0, -1))
    across = direction - 3 * (down + 1) - 1
    codes = ([], [])
    for pair in range(2):
        place = jnp.where(low, slots[2 * pair : 2 * pair + 1], slots[2 * pair + 1 : 2 * pair + 2])
        y, z = (place >> 2) + down, (place & 3) + across
        inside = (direction >= 0) & (y >= 0) & (y < 4) & (z >= 0) & (z < 4)
        wanted = jnp.where(inside, y * 4 + z, -2)
        for found, candidates in zip(codes, ([slots[j : j + 1] for j in range(4)], own_slots)):
            code = jnp.full((1, 128), -1, I32)
            for j in range(4):
                code = jnp.where(wanted == candidates[j], 64 * j + cells, code)
            found.append(code)
    return [jnp.concatenate(code, axis=1) for code in codes]


def coarse_inner(neighbours, sends, table, from_lower, from_upper, hidden1, pre, pre_edge, w_coarse, coarse_pre,
                 codes, taps, conv, fine_slope, coarse_slope):
    coarse_slope[...] = slope(coarse_pre[...])
    cells = table[3:4, :128]
    for row, a, base, payload in ((0, 0, 4, from_lower), (1, 2, 20, from_upper)):
        slots = arrived_slots(payload)
        code = [edge_code(v, cells, base, slots) for v in coarse_slots(neighbours, table, a)]
        codes[row : row + 1, :] = jnp.concatenate(code, axis=1)
        theirs, ours = peer_codes(table, slots, [slot_of(sends, 1 - row, m) for m in range(4)])
        codes[3 + row : 4 + row, :] = theirs
        codes[5 + row : 6 + row, :] = ours
    code = [local_code(v, cells) for v in coarse_slots(neighbours, table, 1)]
    codes[2:3, :] = jnp.concatenate(code, axis=1)
    codes[7:8, :] = jnp.full((1, 256), -1, I32)
    select = onehot(codes[2:3, :], 256)
    conv[...] = coarse_inner_conv(hidden1[...], select, tap_rows(w_coarse), taps)
    for x in range(8):
        value = pre_edge[0] if x == 0 else pre_edge[1] if x == 7 else pre[x]
        fine_slope[x] = slope(value)


def coarse_outer(codes, table, hidden1, from_lower, from_upper, conv, up_back, w_coarse,
                 gated, delta, taps, delta_lower, delta_upper, peer_taps):
    weight = tap_rows(w_coarse)
    spread = onehot(table[10:11, :512], 128)
    edge = []
    for side, payload, own, result in (
        (0, from_lower, hidden1[:, 768:], delta_lower),
        (1, from_upper, hidden1[:, :256], delta_upper),
    ):
        full = mm(payload[...], spread)
        top = full[:64].astype(BF16)
        part = coarse_outer_conv(codes, side, own, top[:, :256], weight, taps, 256 * side)
        edge.append(part)
        select = onehot(codes[3 + side : 4 + side, :], 256)
        rows = mm(jnp.concatenate([top[:, :256], top[:, 256:]], axis=0), select).astype(BF16)
        facing = hidden1[:, :256] if side == 0 else hidden1[:, 768:]
        beyond = mm(facing, onehot(codes[5 + side : 6 + side, :], 256)).astype(BF16)
        order = (rows[64:], rows[:64], beyond) if side == 0 else (beyond, rows[:64], rows[64:])
        for a, plane in enumerate(order):
            put_taps(peer_taps.at[576 * a : 576 * a + 576], 256 * side, plane, COARSE_SHIFTS)
        value = mm(w_coarse[...], peer_taps[:, 256 * side : 256 * side + 256])
        result[...] = ((full[64:, :256] + full[64:, 256:]) * slope(value)).astype(BF16)
    value = conv[...]
    value = jnp.concatenate([value[:, :256] + edge[0], value[:, 256:768], value[:, 768:] + edge[1]], axis=1)
    gated[...] = silu(value).astype(BF16)
    delta[...] = (up_back[...] * slope(value)).astype(BF16)


def tap_gradient(taps, stack, edge_taps, first, last):
    own = nt(taps, stack)
    width = first.shape[1]
    low, high = nt(edge_taps[:, :width], first), nt(edge_taps[:, width:], last)
    return jnp.concatenate([own[:, :64] + low, own[:, 64:128], own[:, 128:] + high], axis=1)


def turn(codes, gated, delta, taps, edge_taps, cot_patch, w_adj, grads, back, delta_taps, stack):
    select = onehot(codes[2:3, :], 256)
    back[...] = coarse_inner_conv(delta[...], select, w_adj[...], delta_taps)
    stack[0:64, 768:1024] = jnp.zeros((64, 256), BF16)
    stack[128:192, 0:256] = jnp.zeros((64, 256), BF16)
    stack[0:64, 0:768] = delta[:, 256:]
    stack[64:128, :] = delta[...]
    stack[128:192, 256:1024] = delta[:, :768]
    of_coarse = tap_gradient(taps[...], stack[...], edge_taps, delta[:, :256], delta[:, 768:])
    of_up = jnp.concatenate([nt(cot_patch[...], gated[...]), jnp.zeros((64, 64), F32)], axis=0)
    put_grads(grads, of_coarse, of_up)


def decode(table, gated, hidden, w_ups, decoded, spread):
    chosen = mm(by_rows(gated[...]), onehot(table[7:8, :1024], 256)).astype(BF16)
    for x in range(4):
        for jl in range(4):
            spread[64 * jl : 64 * jl + 64, 256 * x : 256 * x + 256] = (
                chosen[64 * x : 64 * x + 64, 256 * jl : 256 * jl + 256]
            )
    up = mm(w_ups[...], spread[...])
    compress = onehot(table[6:7, :128], 256)
    low = low_half((64, 128))
    for p in range(2):
        rows = jnp.concatenate([hidden[x, :, 256 * p : 256 * p + 256] for x in range(8)], axis=0)
        own = mm(rows, compress)
        for t in range(4):
            even, odd = [
                own[64 * x : 64 * x + 64] + up[64 * i : 64 * i + 64, 256 * t + 128 * p : 256 * t + 128 * p + 128]
                for i, x in ((0, 2 * t), (1, 2 * t + 1))
            ]
            decoded[2 * p, :, 128 * t : 128 * t + 128] = merge(low, even, odd).astype(BF16)
            decoded[2 * p + 1, :, 128 * t : 128 * t + 128] = merge_high(low, even, odd).astype(BF16)


def finish(core, table, codes, delta, from_lower, from_upper, back, w_adj, coarse_slope, patch, w_dns, fine_slope,
           cot_plane, taps, edge_taps, grads_b, keep, send, coarse_taps, spread, stack, grads):
    weight = w_adj[...]
    low = coarse_outer_conv(codes, 0, delta[:, 768:], from_lower[...], weight, coarse_taps, 0)
    high = coarse_outer_conv(codes, 1, delta[:, :256], from_upper[...], weight, coarse_taps, 256)
    value = back[...]
    value = jnp.concatenate([value[:, :256] + low, value[:, 256:768], value[:, 768:] + high], axis=1)
    down = (value * coarse_slope[...]).astype(BF16)
    of_down = jnp.concatenate([nt(patch[...], down), jnp.zeros((64, 64), F32)], axis=0)
    chosen = mm(by_rows(down), onehot(table[8:9, :2048], 256)).astype(BF16)
    for x in range(4):
        for jl in range(4):
            spread[64 * jl : 64 * jl + 64, 512 * x : 512 * x + 512] = (
                chosen[64 * x : 64 * x + 64, 512 * jl : 512 * jl + 512]
            )
    stack[0:64, 3584:4096] = jnp.zeros((64, 512), BF16)
    stack[128:192, 0:512] = jnp.zeros((64, 512), BF16)
    for half in range(4):
        raised = mm(w_dns[...], spread[:, 512 * half : 512 * half + 512])
        for i in range(2):
            x = 2 * half + i
            total = cot_plane[x].astype(F32) + raised[64 * i : 64 * i + 64]
            fine = (total * fine_slope[x]).astype(BF16)
            for a in range(3):
                plane = x + a - 1
                if 0 <= plane < 8:
                    stack[64 * a : 64 * a + 64, 512 * plane : 512 * plane + 512] = fine
    of_fine = tap_gradient(taps[...], stack[...], edge_taps, stack[64:128, 0:512], stack[64:128, 3584:4096])
    put_grads(grads, of_fine, of_down)
    first = core[0] == 0

    @pl.when(first)
    def _():
        keep[...] = grads[...]
        send[...] = grads_b[...].astype(BF16)

    @pl.when(jnp.logical_not(first))
    def _():
        keep[...] = grads_b[...]
        send[...] = grads[...].astype(BF16)


def put_grads(grads, wide, narrow):
    grads[0:576, :] = wide[:, :128]
    grads[576:1152, :] = jnp.concatenate([wide[:, 128:], narrow], axis=1)


def unfold(factor, core, own, other, grad_fine, grad_down, grad_coarse, grad_up):
    def spell(half, wide, narrow):
        both = jnp.concatenate([half[0:576, :], half[576:1152, :]], axis=1)
        turned = (both.astype(F32) * factor).T
        wide[...] = jnp.concatenate([turned[64 * a : 64 * a + 64, :] for a in range(3)], axis=1)
        narrow[...] = turned[192:256, :512]

    first = core[0] == 0

    @pl.when(first)
    def _():
        spell(own, grad_fine, grad_down)
        spell(other, grad_coarse, grad_up)

    @pl.when(jnp.logical_not(first))
    def _():
        spell(other, grad_fine, grad_down)
        spell(own, grad_coarse, grad_up)


VMEM_SPEC = pl.BlockSpec(memory_space=pltpu.VMEM)
SMEM_SPEC = pl.BlockSpec(memory_space=pltpu.SMEM)
HBM_SPEC = pl.BlockSpec(memory_space=pltpu.HBM)


def call(kernel, name, megabytes, outs, scratch, near, far=(), late=False):
    counts = (len(near), len(far), len(outs), len(scratch), len(far))
    far_outs = [k for k, (away, _, _) in enumerate(outs) if away]

    def body(*refs):
        groups, at = [], 0
        for count in counts:
            groups.append(refs[at : at + count])
            at += count
        near_refs, far_refs, out_refs, own, landed = groups
        staged, (in_sem, out_sem) = refs[at : at + len(far_outs)], refs[at + len(far_outs) :]
        arriving = [pltpu.make_async_copy(s, d, in_sem.at[k]) for k, (s, d) in enumerate(zip(far_refs, landed))]
        for copy in arriving:
            copy.start()
        results = list(out_refs)
        for k, buffer in zip(far_outs, staged):
            results[k] = buffer
        if late:
            kernel([copy.wait for copy in arriving], *near_refs, *landed, *results, *own)
        else:
            for copy in arriving:
                copy.wait()
            kernel(*near_refs, *landed, *results, *own)
        leaving = [
            pltpu.make_async_copy(buffer, out_refs[k], out_sem.at[n])
            for n, (k, buffer) in enumerate(zip(far_outs, staged))
        ]
        for copy in leaving:
            copy.start()
        for copy in leaving:
            copy.wait()

    small = ((4, 26), (2, 16), (1,))
    return pl.pallas_call(
        body,
        name=name,
        out_shape=[jax.ShapeDtypeStruct(shape, kind) for _, shape, kind in outs],
        in_specs=[SMEM_SPEC if x.shape in small else VMEM_SPEC for x in near] + [HBM_SPEC] * len(far),
        out_specs=[HBM_SPEC if away else VMEM_SPEC for away, _, _ in outs],
        scratch_shapes=[pltpu.VMEM(shape, kind) for shape, kind in scratch]
        + [pltpu.VMEM(x.shape, x.dtype) for x in far]
        + [pltpu.VMEM(outs[k][1], outs[k][2]) for k in far_outs]
        + [pltpu.SemaphoreType.DMA((max(len(far), 1),)), pltpu.SemaphoreType.DMA((max(len(far_outs), 1),))],
        compiler_params=pltpu.CompilerParams(vmem_limit_bytes=megabytes * 1024 * 1024),
    )(*near, *far)


def passed_along(block, distance):
    devices = range(lax.axis_size(CHIPS))
    route = [(i - distance, i) for i in devices if i - distance in devices]
    return lax.ppermute(block, CHIPS, route)


def other_core(x):
    return lax.ppermute(x, "core", [(0, 1), (1, 0)])


def dealt(x, axes):
    count = lax.axis_size(axes)
    return lax.all_to_all(x.reshape(count, -1, 128), axes, 0, 0, tiled=True)


def told(x, axes):
    return dealt(jnp.broadcast_to(x, (lax.axis_size(axes), *x.shape)), axes)


def summed(blocks):
    total = blocks[0].astype(F32)
    for k in range(1, blocks.shape[0]):
        total = total + blocks[k].astype(F32)
    return total


def total_over_devices(keep, send):
    x = keep + other_core(send).astype(F32)
    x = summed(dealt(x.astype(BF16), ("y", "x")))
    x = summed(told(x.astype(BF16), "z"))
    return told(x.astype(BF16), ("y", "x")).reshape(keep.shape)


def shards(features, neighbours, send_list, w_fine, w_down, w_coarse, w_up, cotangent):
    feat, cot = features[0], cotangent[0]
    near, sends = neighbours[0], send_list[0, 0]
    core = lax.axis_index("core").astype(I32).reshape(1)
    table = jnp.asarray(TABLE)
    tile = (4, 64, 128)
    face = jax.ShapeDtypeStruct((144, 128), BF16)
    to_upper, to_lower = pl.pallas_call(
        pack_faces,
        name="pack_faces",
        grid=(1,),
        out_shape=[face, face],
        in_specs=[SMEM_SPEC, SMEM_SPEC, pl.BlockSpec(tile, lambda i: (0, 0, 0)), pl.BlockSpec(tile, lambda i: (0, 0, 3))],
        out_specs=[pl.BlockSpec((144, 128), lambda i: (0, 0))] * 2,
        compiler_params=pltpu.CompilerParams(vmem_limit_bytes=60 * 1024 * 1024),
    )(core, sends, feat, feat)
    from_lower, from_upper = passed_along(to_upper, 1), passed_along(to_lower, -1)

    fine = (8, 64, 512)
    pre, edges, up_back, taps0, cot_plane, cot_patch, w_adj, w_ups, w_dns = call(
        fine_inner, "fine_inner", 8,
        [(0, fine, F32), (0, (2, 64, 256), BF16), (0, (64, 1024), F32), (0, (576, 4096), BF16), (0, fine, BF16),
         (0, (512, 1024), BF16), (0, (192, 576), BF16), (0, (128, 256), BF16), (0, (128, 256), BF16)],
        [],
        [near, table, w_fine, w_down, w_coarse, w_up, feat, cot],
    )
    hidden0, patch0, coarse_pre, hidden1, pre_edge, taps0_edge, to_upper, to_lower = call(
        fine_outer, "fine_outer", 4,
        [(0, fine, BF16), (0, (512, 1024), BF16), (0, (64, 1024), F32), (0, (64, 1024), BF16), (0, (2, 64, 512), F32),
         (0, (576, 1024), BF16), (0, (128, 128), BF16), (0, (128, 128), BF16)],
        [],
        [near, table, from_lower, from_upper, edges, pre, w_fine, w_down, up_back],
    )
    low1, high1 = passed_along(to_upper, 1), passed_along(to_lower, -1)
    codes, taps1, conv, fine_slope, coarse_slope = call(
        coarse_inner, "coarse_inner", 4,
        [(0, (8, 256), I32), (0, (576, 1024), BF16), (0, (64, 1024), F32), (0, fine, F32), (0, (64, 1024), F32)],
        [],
        [near, sends, table, from_lower, from_upper, hidden1, pre, pre_edge, w_coarse, coarse_pre],
    )
    gated, delta_up, taps1_edge, low2, high2 = call(
        coarse_outer, "coarse_outer", 5,
        [(0, (64, 1024), BF16), (0, (64, 1024), BF16), (0, (576, 512), BF16), (0, (64, 256), BF16), (0, (64, 256), BF16)],
        [((1728, 512), BF16)],
        [codes, table, hidden1, low1, high1, conv, up_back, w_coarse],
    )
    grads_b, back = call(
        turn, "turn", 5,
        [(0, (1152, 128), F32), (0, (64, 1024), F32)],
        [((576, 1024), BF16), ((192, 1024), BF16)],
        [codes, gated, delta_up, taps1, taps1_edge, cot_patch, w_adj],
    )
    (decoded,) = call(
        decode, "decode", 5, [(0, (4, 64, 512), BF16)], [((256, 1024), BF16)], [table, gated, hidden0, w_ups],
    )
    keep, send = call(
        finish, "finish", 8,
        [(0, (1152, 128), F32), (0, (1152, 128), BF16)],
        [((576, 512), BF16), ((256, 2048), BF16), ((192, 4096), BF16), ((1152, 128), F32)],
        [core, table, codes, delta_up, low2, high2, back, w_adj, coarse_slope, patch0, w_dns, fine_slope, cot_plane, taps0,
         taps0_edge, grads_b],
    )
    total = total_over_devices(keep, send)
    factor = 1.0 / math.sqrt(lax.axis_size(AXES) * 4 * 512)
    outs = call(
        lambda *refs: unfold(factor, *refs), "unfold", 3,
        [(0, w_fine.shape, F32), (0, w_down.shape, F32), (0, w_coarse.shape, F32), (0, w_up.shape, F32)], [], [core, total, other_core(total)],
    )
    return (decoded[None], *outs)


def solution(mesh):
    chips = mesh.devices.shape[0]
    x = min(4, chips)
    y = min(4, chips // x)
    grid = Mesh(mesh.devices.reshape(chips // (x * y), y, x, -1), AXES)
    in_specs = (
        P("core", CHIPS, None, None),
        P("core", CHIPS, None),
        P("core", CHIPS, None, None),
        P(),
        P(),
        P(),
        P(),
        P("core", CHIPS, None, None),
    )
    out_specs = (P("core", CHIPS, None, None), P(), P(), P(), P())
    return jax.shard_map(shards, mesh=grid, in_specs=in_specs, out_specs=out_specs, check_vma=False)
```

```python
import math

import jax
import jax.numpy as jnp
import numpy as np
from jax import lax
from jax.experimental import pallas as pl
from jax.experimental.pallas import tpu as pltpu
from jax.sharding import Mesh
from jax.sharding import PartitionSpec as P

F32 = jnp.float32
BF16 = jnp.bfloat16
I32 = jnp.int32
CHIPS = ("z", "y", "x")
AXES = ("z", "y", "x", "core")
FINE_SHIFTS = [10 * (c - 1) + (e - 1) for c in range(3) for e in range(3)]
COARSE_SHIFTS = [6 * (c - 1) + (e - 1) for c in range(3) for e in range(3)]


def lane_tables():
    table = np.full((16, 2048), -1, np.int32)
    t = np.arange(128)
    y, z, inside = t // 10 - 1, t % 10 - 1, t < 100
    c, e = np.where(y < 0, 0, np.where(y >= 8, 2, 1)), np.where(z < 0, 0, np.where(z >= 8, 2, 1))
    table[0, :128] = np.where(inside, 3 * c + e, -1)
    table[1, :128] = np.where(inside, (y - 8 * (c - 1)) * 8 + (z - 8 * (e - 1)), 0)
    own = inside & (c == 1) & (e == 1)
    for b in range(4):
        table[4, 128 * b : 128 * b + 128] = np.where(own, 64 * b + y * 8 + z, -1)
    u = np.arange(64)
    cy, cz, cin = u // 6 - 1, u % 6 - 1, u < 36
    cc, ce = np.where(cy < 0, 0, np.where(cy >= 4, 2, 1)), np.where(cz < 0, 0, np.where(cz >= 4, 2, 1))
    for b in range(2):
        at = slice(64 * b, 64 * b + 64)
        table[2, at] = np.where(cin, 3 * cc + ce, -1)
        table[3, at] = np.where(cin, 6 * (cy - 4 * (cc - 1) + 1) + cz - 4 * (ce - 1) + 1, 0)
    cown = cin & (cc == 1) & (ce == 1)
    w = np.arange(64)
    for j in range(2):
        for l in range(2):
            for b in range(2):
                at = (2 * j + l) * 128 + 64 * b
                rows = 128 * b + 10 * (2 * cy + j + 1) + 2 * cz + l + 1
                table[5, at : at + 64] = np.where(cown, rows, -1)
            for b in range(4):
                ny, nz = w // 8, w % 8
                hit = (ny % 2 == j) & (nz % 2 == l)
                at = (2 * j + l) * 256 + 64 * b
                table[7, at : at + 64] = np.where(hit, 64 * b + 6 * (ny // 2 + 1) + nz // 2 + 1, -1)
                hit = own & (y % 2 == j) & (z % 2 == l)
                at = (2 * j + l) * 512 + 128 * b
                table[8, at : at + 128] = np.where(hit, 64 * b + 6 * (y // 2 + 1) + z // 2 + 1, -1)
    real = np.flatnonzero(cown)
    for half in range(2):
        for b in range(4):
            table[9, 64 * half + 16 * b : 64 * half + 16 * b + 16] = 256 * half + 64 * b + real
            table[10, 256 * half + 64 * b + real] = 64 * half + 16 * b + np.arange(16)
    for b in range(2):
        table[6, 64 * b : 64 * b + 64] = 128 * b + 10 * (w // 8 + 1) + w % 8 + 1
    return table


TABLE = lane_tables()


def mm(a, b):
    return jnp.dot(a, b, preferred_element_type=F32)


def nt(a, b):
    return lax.dot_general(a, b, (((1,), (1,)), ((), ())), preferred_element_type=F32)


def roll(v, shift):
    return pltpu.roll(v, shift % 128, 1)


def onehot(code, rows):
    hit = lax.broadcasted_iota(I32, (rows, code.shape[1]), 0) == code
    return jnp.where(hit, 1.0, 0.0).astype(BF16)


def low_half(shape):
    return lax.broadcasted_iota(I32, shape, 1) < 64


def merge(low, first, second):
    return jnp.where(low, first, roll(second, 64))


def merge_high(low, first, second):
    return jnp.where(low, roll(first, 64), second)


def sigmoid(v):
    return 1.0 / (1.0 + jnp.exp(-v))


def silu(v):
    return v / (1.0 + jnp.exp(-v))


def slope(v):
    s = sigmoid(v)
    return s * (1.0 + v * (1.0 - s))


def raw_slots(neighbours, a, block, direction):
    found = jnp.full(direction.shape, -1, I32)
    for j in range(9):
        k = 9 * a + j
        entry = block if k == 13 else neighbours[block, k - (k > 13)]
        found = jnp.where(direction == j, entry, found)
    return found


def local_code(slots, cells):
    return jnp.where(slots >= 0, slots * 64 + cells, -1)


def edge_code(slots, cells, base, remote_slots):
    code = jnp.where((slots >= 0) & (slots < 4), slots * 64 + cells, -1)
    reach = (slots >= base) & (slots < base + 16)
    for j in range(4):
        hit = reach & (slots - base == remote_slots[j : j + 1])
        code = jnp.where(hit, 256 + j * 64 + cells, code)
    return code


def fine_slots(neighbours, table, a):
    direction = table[0:1, :128]
    return [raw_slots(neighbours, a, b, direction) for b in range(4)]


def coarse_slots(neighbours, table, a):
    direction = table[2:3, :128]
    low = low_half((1, 128))
    per_block = [raw_slots(neighbours, a, b, direction) for b in range(4)]
    return [jnp.where(low, per_block[0], per_block[1]), jnp.where(low, per_block[2], per_block[3])]


def arrived_slots(payload):
    return payload[128:144, :].astype(F32).astype(I32)


def tap_rows(w_ref):
    return jnp.concatenate([w_ref[:, 576 * a : 576 * a + 576] for a in range(3)], axis=0)


def put_taps(dst, at, plane, shifts):
    for s in range(plane.shape[1] // 128):
        piece = plane[:, 128 * s : 128 * s + 128]
        for j, shift in enumerate(shifts):
            moved = piece if shift == 0 else roll(piece, -shift)
            dst[64 * j : 64 * j + 64, at + 128 * s : at + 128 * s + 128] = moved


def natural_planes(ref):
    low = low_half((64, 128))
    planes = []
    for t in range(4):
        tiles = [ref[b, :, 128 * t : 128 * t + 128] for b in range(4)]
        planes.append(jnp.concatenate([merge(low, tiles[2 * p], tiles[2 * p + 1]) for p in range(2)], axis=1))
        planes.append(jnp.concatenate([merge_high(low, tiles[2 * p], tiles[2 * p + 1]) for p in range(2)], axis=1))
    return planes


def transposed_blocks(w, order):
    wt = w.astype(F32).T
    return jnp.concatenate([wt[64 * k : 64 * k + 64, :] for k in order], axis=1).astype(BF16)


def slot_of(sends, side, block):
    slot = jnp.int32(-1)
    for s in range(16):
        slot = jnp.where(sends[side, s] == block, s, slot)
    return slot


def pack_faces(core, sends, low_tile, high_tile, to_upper, to_lower):
    low = low_half((64, 128))
    for p in range(2):
        to_upper[64 * p : 64 * p + 64, :] = merge_high(low, high_tile[2 * p], high_tile[2 * p + 1])
        to_lower[64 * p : 64 * p + 64, :] = merge(low, low_tile[2 * p], low_tile[2 * p + 1])
    rows = lax.broadcasted_iota(I32, (16, 128), 0)
    for side, out in ((0, to_upper), (1, to_lower)):
        slots = jnp.full((16, 128), -1, I32)
        for j in range(4):
            slots = jnp.where(rows == j, slot_of(sends, side, j), slots)
        out[128:144, :] = slots.astype(F32).astype(BF16)


def fine_inner(neighbours, table, w_fine, w_down, w_coarse, w_up, feat, cot,
               pre, edges, up_back, ext, cot_plane, cot_patch, w_adj, w_ups, w_dns, taps):
    planes = natural_planes(feat)
    edges[0], edges[1] = planes[0], planes[7]
    cells = table[1:2, :128]
    code = jnp.concatenate([local_code(v, cells) for v in fine_slots(neighbours, table, 1)], axis=1)
    whole = mm(jnp.concatenate(planes, axis=0), onehot(code, 256)).astype(BF16)
    weight = tap_rows(w_fine)
    for x in range(8):
        plane = whole[64 * x : 64 * x + 64]
        ext[x] = plane
        put_taps(taps, 512 * x, plane, FINE_SHIFTS)
    for x in range(8):
        part = mm(weight, taps[:, 512 * x : 512 * x + 512])
        for a in range(3):
            out = x + 1 - a
            if 0 <= out < 8:
                piece = part[64 * a : 64 * a + 64]
                if x == max(out - 1, 0):
                    pre[out] = piece
                else:
                    pre[out] += piece
    placed = mm(jnp.concatenate(natural_planes(cot), axis=0), onehot(table[4:5, :512], 256)).astype(BF16)
    for x in range(8):
        cot_plane[x] = placed[64 * x : 64 * x + 64]
    down = onehot(table[5:6, :512], 256)
    for p in range(2):
        put_patches(cot_patch, mm(placed[:, 256 * p : 256 * p + 256], down).astype(BF16), p)
    up_back[...] = mm(w_up[...], cot_patch[...])
    for a in range(3):
        order = [(2 - a) * 9 + 8 - j for j in range(9)]
        w_adj[64 * a : 64 * a + 64, :] = transposed_blocks(w_coarse[...], order)
    for i in range(2):
        w_ups[64 * i : 64 * i + 64, :] = transposed_blocks(w_up[...], range(4 * i, 4 * i + 4))
        w_dns[64 * i : 64 * i + 64, :] = transposed_blocks(w_down[...], range(4 * i, 4 * i + 4))


def put_patches(dst, selected, pair):
    for x in range(8):
        for jl in range(4):
            at = ((x % 2) * 4 + jl) * 64
            lane = (x // 2) * 256 + pair * 128
            dst[at : at + 64, lane : lane + 128] = selected[64 * x : 64 * x + 64, 128 * jl : 128 * jl + 128]


def boundary(table, hidden1, up_back, edge, inner):
    exact = up_back[:, 256 * edge : 256 * edge + 256]
    high = exact.astype(BF16)
    low = (exact - high.astype(F32)).astype(BF16)
    top = jnp.concatenate([hidden1[:, 256 * p : 256 * p + 256] for p in (edge, inner)], axis=1)
    both = jnp.concatenate([top, jnp.concatenate([high, low], axis=1)], axis=0)
    return mm(both, onehot(table[9:10, :128], 512)).astype(BF16)


def fine_outer(neighbours, table, from_lower, from_upper, edges, pre, w_fine, w_down, up_back,
               hidden, patch, coarse_pre, hidden1, pre_edge, ext_edge, to_upper, to_lower, taps):
    cells = table[1:2, :128]
    weight = tap_rows(w_fine)
    for side, a, base, payload in ((0, 0, 4, from_lower), (1, 2, 20, from_upper)):
        slots = arrived_slots(payload)
        code = jnp.concatenate([edge_code(v, cells, base, slots) for v in fine_slots(neighbours, table, a)], axis=1)
        pool = jnp.concatenate([edges[1 - side], payload[0:64, :], payload[64:128, :]], axis=1)
        plane = mm(pool, onehot(code, 512)).astype(BF16)
        ext_edge[side] = plane
        put_taps(taps, 512 * side, plane, FINE_SHIFTS)
        part = mm(weight[64 * a : 64 * a + 64], taps[:, 512 * side : 512 * side + 512])
        pre_edge[side] = pre[7 * side] + part
    for x in range(8):
        value = pre_edge[0] if x == 0 else pre_edge[1] if x == 7 else pre[x]
        hidden[x] = silu(value).astype(BF16)
    down = onehot(table[5:6, :512], 256)
    for p in range(2):
        rows = jnp.concatenate([hidden[x, :, 256 * p : 256 * p + 256] for x in range(8)], axis=0)
        put_patches(patch, mm(rows, down).astype(BF16), p)
    value = mm(w_down[...], patch[...])
    coarse_pre[...] = value
    value = silu(value).astype(BF16)
    hidden1[...] = value
    exact = up_back[...]
    to_upper[...] = boundary(table, value, exact, 3, 2)
    to_lower[...] = boundary(table, value, exact, 0, 1)


def by_rows(v):
    return jnp.concatenate([v[:, 256 * x : 256 * x + 256] for x in range(4)], axis=0)


def coarse_inner_conv(field, select, weight, taps, ext):
    whole = mm(by_rows(field), select).astype(BF16)
    for x in range(4):
        plane = whole[64 * x : 64 * x + 64]
        if ext is not None:
            ext[:, 256 * x : 256 * x + 256] = plane
        put_taps(taps, 256 * x, plane, COARSE_SHIFTS)
    part = mm(weight, taps[:, :1024])
    sums = []
    for x in range(4):
        total = part[64:128, 256 * x : 256 * x + 256]
        if x > 0:
            total = total + part[0:64, 256 * x - 256 : 256 * x]
        if x < 3:
            total = total + part[128:192, 256 * x + 256 : 256 * x + 512]
        sums.append(total)
    return jnp.concatenate(sums, axis=1)


def coarse_outer_conv(codes, side, own_plane, arrived, weight, taps, at):
    pool = jnp.concatenate([own_plane, arrived], axis=1)
    plane = mm(pool, onehot(codes[side : side + 1, :], 512)).astype(BF16)
    put_taps(taps, at, plane, COARSE_SHIFTS)
    return mm(weight[128 * side : 128 * side + 64], taps[:, at : at + 256]), plane


def peer_codes(table, slots, own_slots):
    direction, cells = table[2:3, :128], table[3:4, :128]
    low = low_half((1, 128))
    down = jnp.where(direction >= 6, 1, jnp.where(direction >= 3, 0, -1))
    across = direction - 3 * (down + 1) - 1
    codes = ([], [])
    for pair in range(2):
        place = jnp.where(low, slots[2 * pair : 2 * pair + 1], slots[2 * pair + 1 : 2 * pair + 2])
        y, z = (place >> 2) + down, (place & 3) + across
        inside = (direction >= 0) & (y >= 0) & (y < 4) & (z >= 0) & (z < 4)
        wanted = jnp.where(inside, y * 4 + z, -2)
        for found, candidates in zip(codes, ([slots[j : j + 1] for j in range(4)], own_slots)):
            code = jnp.full((1, 128), -1, I32)
            for j in range(4):
                code = jnp.where(wanted == candidates[j], 64 * j + cells, code)
            found.append(code)
    return [jnp.concatenate(code, axis=1) for code in codes]


def coarse_inner(neighbours, sends, table, from_lower, from_upper, hidden1, pre, pre_edge, w_coarse, coarse_pre,
                 codes, ext, conv, fine_slope, coarse_slope, taps):
    coarse_slope[...] = slope(coarse_pre[...])
    cells = table[3:4, :128]
    for row, a, base, payload in ((0, 0, 4, from_lower), (1, 2, 20, from_upper)):
        slots = arrived_slots(payload)
        code = [edge_code(v, cells, base, slots) for v in coarse_slots(neighbours, table, a)]
        codes[row : row + 1, :] = jnp.concatenate(code, axis=1)
        theirs, ours = peer_codes(table, slots, [slot_of(sends, 1 - row, m) for m in range(4)])
        codes[3 + row : 4 + row, :] = theirs
        codes[5 + row : 6 + row, :] = ours
    code = [local_code(v, cells) for v in coarse_slots(neighbours, table, 1)]
    codes[2:3, :] = jnp.concatenate(code, axis=1)
    codes[7:8, :] = jnp.full((1, 256), -1, I32)
    select = onehot(codes[2:3, :], 256)
    conv[...] = coarse_inner_conv(hidden1[...], select, tap_rows(w_coarse), taps, ext)
    for x in range(8):
        value = pre_edge[0] if x == 0 else pre_edge[1] if x == 7 else pre[x]
        fine_slope[x] = slope(value)


def coarse_outer(codes, table, hidden1, from_lower, from_upper, conv, up_back, w_coarse,
                 gated, delta, ext_edge, delta_lower, delta_upper, taps, peer_taps):
    weight = tap_rows(w_coarse)
    spread = onehot(table[10:11, :512], 128)
    edge = []
    for side, payload, own, result in (
        (0, from_lower, hidden1[:, 768:], delta_lower),
        (1, from_upper, hidden1[:, :256], delta_upper),
    ):
        full = mm(payload[...], spread)
        top = full[:64].astype(BF16)
        part, ext_edge[side] = coarse_outer_conv(codes, side, own, top[:, :256], weight, taps, 256 * side)
        edge.append(part)
        select = onehot(codes[3 + side : 4 + side, :], 256)
        rows = mm(jnp.concatenate([top[:, :256], top[:, 256:]], axis=0), select).astype(BF16)
        facing = hidden1[:, :256] if side == 0 else hidden1[:, 768:]
        beyond = mm(facing, onehot(codes[5 + side : 6 + side, :], 256)).astype(BF16)
        order = (rows[64:], rows[:64], beyond) if side == 0 else (beyond, rows[:64], rows[64:])
        for a, plane in enumerate(order):
            put_taps(peer_taps.at[576 * a : 576 * a + 576], 256 * side, plane, COARSE_SHIFTS)
        value = mm(w_coarse[...], peer_taps[:, 256 * side : 256 * side + 256])
        result[...] = ((full[64:, :256] + full[64:, 256:]) * slope(value)).astype(BF16)
    value = conv[...]
    value = jnp.concatenate([value[:, :256] + edge[0], value[:, 256:768], value[:, 768:] + edge[1]], axis=1)
    gated[...] = silu(value).astype(BF16)
    delta[...] = (up_back[...] * slope(value)).astype(BF16)


def turn(codes, gated, delta, ext, ext_edge, cot_patch, w_adj, grads, back, taps, stack):
    select = onehot(codes[2:3, :], 256)
    back[...] = coarse_inner_conv(delta[...], select, w_adj[...], taps, None)
    put_taps(taps, 0, ext_edge[0], COARSE_SHIFTS)
    for x in range(4):
        put_taps(taps, 256 + 256 * x, ext[:, 256 * x : 256 * x + 256], COARSE_SHIFTS)
    put_taps(taps, 1280, ext_edge[1], COARSE_SHIFTS)
    stack[...] = jnp.zeros(stack.shape, BF16)
    for a in range(3):
        stack[64 * a : 64 * a + 64, 256 * a : 256 * a + 1024] = delta[...]
    of_coarse = nt(taps[...], stack[...])
    of_up = jnp.concatenate([nt(cot_patch[...], gated[...]), jnp.zeros((64, 64), F32)], axis=0)
    put_grads(grads, of_coarse, of_up)


def decode(table, gated, hidden, w_ups, decoded, spread):
    chosen = mm(by_rows(gated[...]), onehot(table[7:8, :1024], 256)).astype(BF16)
    for x in range(4):
        for jl in range(4):
            spread[64 * jl : 64 * jl + 64, 256 * x : 256 * x + 256] = (
                chosen[64 * x : 64 * x + 64, 256 * jl : 256 * jl + 256]
            )
    up = mm(w_ups[...], spread[...])
    compress = onehot(table[6:7, :128], 256)
    low = low_half((64, 128))
    for p in range(2):
        rows = jnp.concatenate([hidden[x, :, 256 * p : 256 * p + 256] for x in range(8)], axis=0)
        own = mm(rows, compress)
        for t in range(4):
            even, odd = [
                own[64 * x : 64 * x + 64] + up[64 * i : 64 * i + 64, 256 * t + 128 * p : 256 * t + 128 * p + 128]
                for i, x in ((0, 2 * t), (1, 2 * t + 1))
            ]
            decoded[2 * p, :, 128 * t : 128 * t + 128] = merge(low, even, odd).astype(BF16)
            decoded[2 * p + 1, :, 128 * t : 128 * t + 128] = merge_high(low, even, odd).astype(BF16)


def finish(core, table, codes, delta, from_lower, from_upper, back, w_adj, coarse_slope, patch, w_dns, fine_slope,
           cot_plane, ext, ext_edge, grads_b, keep, send, coarse_taps, spread, taps, stack, grads):
    weight = w_adj[...]
    low, _ = coarse_outer_conv(codes, 0, delta[:, 768:], from_lower[...], weight, coarse_taps, 0)
    high, _ = coarse_outer_conv(codes, 1, delta[:, :256], from_upper[...], weight, coarse_taps, 256)
    value = back[...]
    value = jnp.concatenate([value[:, :256] + low, value[:, 256:768], value[:, 768:] + high], axis=1)
    down = (value * coarse_slope[...]).astype(BF16)
    of_down = jnp.concatenate([nt(patch[...], down), jnp.zeros((64, 64), F32)], axis=0)
    chosen = mm(by_rows(down), onehot(table[8:9, :2048], 256)).astype(BF16)
    for x in range(4):
        for jl in range(4):
            spread[64 * jl : 64 * jl + 64, 512 * x : 512 * x + 512] = (
                chosen[64 * x : 64 * x + 64, 512 * jl : 512 * jl + 512]
            )
    for a in range(3):
        for plane in range(10):
            if not 0 <= plane - a < 8:
                stack[64 * a : 64 * a + 64, 512 * plane : 512 * plane + 512] = jnp.zeros((64, 512), BF16)
    for half in range(4):
        raised = mm(w_dns[...], spread[:, 512 * half : 512 * half + 512])
        for i in range(2):
            x = 2 * half + i
            total = cot_plane[x].astype(F32) + raised[64 * i : 64 * i + 64]
            fine = (total * fine_slope[x]).astype(BF16)
            for a in range(3):
                at = 512 * (x + a)
                stack[64 * a : 64 * a + 64, at : at + 512] = fine
    put_taps(taps, 0, ext_edge[0], FINE_SHIFTS)
    for x in range(8):
        put_taps(taps, 512 * x + 512, ext[x], FINE_SHIFTS)
    put_taps(taps, 4608, ext_edge[1], FINE_SHIFTS)
    put_grads(grads, nt(taps[...], stack[...]), of_down)
    first = core[0] == 0

    @pl.when(first)
    def _():
        keep[...] = grads[...]
        send[...] = grads_b[...].astype(BF16)

    @pl.when(jnp.logical_not(first))
    def _():
        keep[...] = grads_b[...]
        send[...] = grads[...].astype(BF16)


def put_grads(grads, wide, narrow):
    grads[0:576, :] = wide[:, :128]
    grads[576:1152, :] = jnp.concatenate([wide[:, 128:], narrow], axis=1)


def unfold(factor, core, own, other, grad_fine, grad_down, grad_coarse, grad_up):
    def spell(half, wide, narrow):
        both = jnp.concatenate([half[0:576, :], half[576:1152, :]], axis=1)
        turned = (both.astype(F32) * factor).T
        wide[...] = jnp.concatenate([turned[64 * a : 64 * a + 64, :] for a in range(3)], axis=1)
        narrow[...] = turned[192:256, :512]

    first = core[0] == 0

    @pl.when(first)
    def _():
        spell(own, grad_fine, grad_down)
        spell(other, grad_coarse, grad_up)

    @pl.when(jnp.logical_not(first))
    def _():
        spell(other, grad_fine, grad_down)
        spell(own, grad_coarse, grad_up)


VMEM_SPEC = pl.BlockSpec(memory_space=pltpu.VMEM)
SMEM_SPEC = pl.BlockSpec(memory_space=pltpu.SMEM)
HBM_SPEC = pl.BlockSpec(memory_space=pltpu.HBM)


def call(kernel, name, megabytes, outs, scratch, near, far=(), late=False):
    counts = (len(near), len(far), len(outs), len(scratch), len(far))
    far_outs = [k for k, (away, _, _) in enumerate(outs) if away]

    def body(*refs):
        groups, at = [], 0
        for count in counts:
            groups.append(refs[at : at + count])
            at += count
        near_refs, far_refs, out_refs, own, landed = groups
        staged, (in_sem, out_sem) = refs[at : at + len(far_outs)], refs[at + len(far_outs) :]
        arriving = [pltpu.make_async_copy(s, d, in_sem.at[k]) for k, (s, d) in enumerate(zip(far_refs, landed))]
        for copy in arriving:
            copy.start()
        results = list(out_refs)
        for k, buffer in zip(far_outs, staged):
            results[k] = buffer
        if late:
            kernel([copy.wait for copy in arriving], *near_refs, *landed, *results, *own)
        else:
            for copy in arriving:
                copy.wait()
            kernel(*near_refs, *landed, *results, *own)
        leaving = [
            pltpu.make_async_copy(buffer, out_refs[k], out_sem.at[n])
            for n, (k, buffer) in enumerate(zip(far_outs, staged))
        ]
        for copy in leaving:
            copy.start()
        for copy in leaving:
            copy.wait()

    small = ((4, 26), (2, 16), (1,))
    return pl.pallas_call(
        body,
        name=name,
        out_shape=[jax.ShapeDtypeStruct(shape, kind) for _, shape, kind in outs],
        in_specs=[SMEM_SPEC if x.shape in small else VMEM_SPEC for x in near] + [HBM_SPEC] * len(far),
        out_specs=[HBM_SPEC if away else VMEM_SPEC for away, _, _ in outs],
        scratch_shapes=[pltpu.VMEM(shape, kind) for shape, kind in scratch]
        + [pltpu.VMEM(x.shape, x.dtype) for x in far]
        + [pltpu.VMEM(outs[k][1], outs[k][2]) for k in far_outs]
        + [pltpu.SemaphoreType.DMA((max(len(far), 1),)), pltpu.SemaphoreType.DMA((max(len(far_outs), 1),))],
        compiler_params=pltpu.CompilerParams(vmem_limit_bytes=megabytes * 1024 * 1024),
    )(*near, *far)


def passed_along(block, distance):
    devices = range(lax.axis_size(CHIPS))
    route = [(i - distance, i) for i in devices if i - distance in devices]
    return lax.ppermute(block, CHIPS, route)


def other_core(x):
    return lax.ppermute(x, "core", [(0, 1), (1, 0)])


def dealt(x, axes):
    count = lax.axis_size(axes)
    return lax.all_to_all(x.reshape(count, -1, 128), axes, 0, 0, tiled=True)


def told(x, axes):
    return dealt(jnp.broadcast_to(x, (lax.axis_size(axes), *x.shape)), axes)


def summed(blocks):
    total = blocks[0].astype(F32)
    for k in range(1, blocks.shape[0]):
        total = total + blocks[k].astype(F32)
    return total


def total_over_devices(keep, send):
    x = keep + other_core(send).astype(F32)
    x = summed(dealt(x.astype(BF16), ("y", "x")))
    x = summed(told(x.astype(BF16), "z"))
    return told(x.astype(BF16), ("y", "x")).reshape(keep.shape)


def shards(features, neighbours, send_list, w_fine, w_down, w_coarse, w_up, cotangent):
    feat, cot = features[0], cotangent[0]
    near, sends = neighbours[0], send_list[0, 0]
    core = lax.axis_index("core").astype(I32).reshape(1)
    table = jnp.asarray(TABLE)
    tile = (4, 64, 128)
    face = jax.ShapeDtypeStruct((144, 128), BF16)
    to_upper, to_lower = pl.pallas_call(
        pack_faces,
        name="pack_faces",
        grid=(1,),
        out_shape=[face, face],
        in_specs=[SMEM_SPEC, SMEM_SPEC, pl.BlockSpec(tile, lambda i: (0, 0, 0)), pl.BlockSpec(tile, lambda i: (0, 0, 3))],
        out_specs=[pl.BlockSpec((144, 128), lambda i: (0, 0))] * 2,
        compiler_params=pltpu.CompilerParams(vmem_limit_bytes=60 * 1024 * 1024),
    )(core, sends, feat, feat)
    from_lower, from_upper = passed_along(to_upper, 1), passed_along(to_lower, -1)

    fine = (8, 64, 512)
    pre, edges, up_back, ext0, cot_plane, cot_patch, w_adj, w_ups, w_dns = call(
        fine_inner, "fine_inner", 8,
        [(0, fine, F32), (0, (2, 64, 256), BF16), (0, (64, 1024), F32), (0, fine, BF16), (0, fine, BF16),
         (0, (512, 1024), BF16), (0, (192, 576), BF16), (0, (128, 256), BF16), (0, (128, 256), BF16)],
        [((576, 4096), BF16)],
        [near, table, w_fine, w_down, w_coarse, w_up, feat, cot],
    )
    hidden0, patch0, coarse_pre, hidden1, pre_edge, ext0_edge, to_upper, to_lower = call(
        fine_outer, "fine_outer", 4,
        [(0, fine, BF16), (0, (512, 1024), BF16), (0, (64, 1024), F32), (0, (64, 1024), BF16), (0, (2, 64, 512), F32),
         (0, (2, 64, 512), BF16), (0, (128, 128), BF16), (0, (128, 128), BF16)],
        [((576, 1024), BF16)],
        [near, table, from_lower, from_upper, edges, pre, w_fine, w_down, up_back],
    )
    low1, high1 = passed_along(to_upper, 1), passed_along(to_lower, -1)
    codes, ext1, conv, fine_slope, coarse_slope = call(
        coarse_inner, "coarse_inner", 4,
        [(0, (8, 256), I32), (0, (64, 1024), BF16), (0, (64, 1024), F32), (0, fine, F32), (0, (64, 1024), F32)],
        [((576, 1024), BF16)],
        [near, sends, table, from_lower, from_upper, hidden1, pre, pre_edge, w_coarse, coarse_pre],
    )
    gated, delta_up, ext1_edge, low2, high2 = call(
        coarse_outer, "coarse_outer", 5,
        [(0, (64, 1024), BF16), (0, (64, 1024), BF16), (0, (2, 64, 256), BF16), (0, (64, 256), BF16), (0, (64, 256), BF16)],
        [((576, 512), BF16), ((1728, 512), BF16)],
        [codes, table, hidden1, low1, high1, conv, up_back, w_coarse],
    )
    grads_b, back = call(
        turn, "turn", 6,
        [(0, (1152, 128), F32), (0, (64, 1024), F32)],
        [((576, 1536), BF16), ((192, 1536), BF16)],
        [codes, gated, delta_up, ext1, ext1_edge, cot_patch, w_adj],
    )
    (decoded,) = call(
        decode, "decode", 6, [(0, (4, 64, 512), BF16)], [((256, 1024), BF16)], [table, gated, hidden0, w_ups],
    )
    keep, send = call(
        finish, "finish", 12,
        [(0, (1152, 128), F32), (0, (1152, 128), BF16)],
        [((576, 512), BF16), ((256, 2048), BF16), ((576, 5120), BF16), ((192, 5120), BF16), ((1152, 128), F32)],
        [core, table, codes, delta_up, low2, high2, back, w_adj, coarse_slope, patch0, w_dns, fine_slope, cot_plane, ext0,
         ext0_edge, grads_b],
    )
    total = total_over_devices(keep, send)
    factor = 1.0 / math.sqrt(lax.axis_size(AXES) * 4 * 512)
    outs = call(
        lambda *refs: unfold(factor, *refs), "unfold", 3,
        [(0, w_fine.shape, F32), (0, w_down.shape, F32), (0, w_coarse.shape, F32), (0, w_up.shape, F32)], [], [core, total, other_core(total)],
    )
    return (decoded[None], *outs)


def solution(mesh):
    chips = mesh.devices.shape[0]
    x = min(4, chips)
    y = min(4, chips // x)
    grid = Mesh(mesh.devices.reshape(chips // (x * y), y, x, -1), AXES)
    in_specs = (
        P("core", CHIPS, None, None),
        P("core", CHIPS, None),
        P("core", CHIPS, None, None),
        P(),
        P(),
        P(),
        P(),
        P("core", CHIPS, None, None),
    )
    out_specs = (P("core", CHIPS, None, None), P(), P(), P(), P())
    return jax.shard_map(shards, mesh=grid, in_specs=in_specs, out_specs=out_specs, check_vma=False)
```
